512 devices in a mesh: sub: 64 (over z, y), tm: 8 (over x, core).
Axes of the slice: x: 4, y: 8, z: 8, core: 2. Of those that a mesh axis runs over, the one named last changes fastest.
Arguments:
- data: bfloat16 [1, 16384, 2048], P(None, 'sub', 'tm'), may hold values from -6 to 6
- delays: int32 [16384], P('sub'), may hold values from 0 to 15, as said below
- offsets: int32 [2048, 1024], P('sub'), may hold values from 0 to 96, as said below
- widths: int32 [8], replicated, may hold values from 1 to 128, as said below
Outputs:
- boxcars: float32 [2048, 1, 8, 2048], P('sub', None, None, 'tm')
The draws below stay inside these ranges and needn't reach their ends.
Inputs may be any that keep to these rules, and one draw needn't show every extreme that they name: `delays`: some channel has delay 16 - 1. `offsets`: some entry equals 96 and some entry equals 0. `widths`: some entry equals 128.
All inputs are finite; a program needn't handle non-finite values.
Results may differ from the reference program's by a relative error of at most 0.0048.
Values may be sent and summed in bfloat16 or wider, within the bound.
A program may use at most 64 MiB of HBM per device.

```python
import math
import jax
import jax.numpy as jnp
from jax import lax

NCHAN = 16384
NSUB = 1024
NDM = 2048
NW = 8
WMAX = 128
DCH = 16
OMAX = 96
BEAMS = 1
T_TOTAL = 2048


def draw_delays(key, part):
    first, second_operand = jax.random.split(key, 2)
    values = jax.random.randint(first, (NCHAN,), 0, DCH, dtype=jnp.int32)
    target = jax.random.randint(second_operand, (), 0, NCHAN, dtype=jnp.int32)
    return values.at[target].set(DCH - 1)


def draw_offsets(key, part):
    first, second_operand, third, fourth, fifth = jax.random.split(jax.random.fold_in(key, 17), 5)
    dm_codes = jax.random.randint(first, (NDM,), 0, OMAX + 1, dtype=jnp.int32)
    band_codes = jax.random.randint(second_operand, (NSUB,), 0, 1025, dtype=jnp.int32)
    jitter_top = max(2, OMAX // 16)
    jitter = jax.random.randint(third, (NDM, NSUB), 0, jitter_top + 1, dtype=jnp.int32)
    values = dm_codes[:, None] * band_codes[None, :] // 1024 + jitter
    values = jnp.minimum(values, OMAX)
    top_row = jax.random.randint(fourth, (), 0, NDM, dtype=jnp.int32)
    top_col = jax.random.randint(fifth, (), 0, NSUB, dtype=jnp.int32)
    low_row = (top_row + 1) % NDM
    values = values.at[low_row, top_col].set(0)
    values = values.at[top_row, top_col].set(OMAX)
    return values


def draw_widths(key, part):
    first, second_operand = jax.random.split(jax.random.fold_in(key, 29), 2)
    values = jax.random.randint(first, (NW,), 1, WMAX + 1, dtype=jnp.int32)
    target = jax.random.randint(second_operand, (), 0, NW, dtype=jnp.int32)
    return values.at[target].set(WMAX)


def steps_of(stream_key, extent, shards, low, largest):
    gain = 1.0
    for axis_at, parts in shards:
        heights = jax.random.uniform(jax.random.fold_in(jax.random.fold_in(stream_key, 6), axis_at), (parts,), jnp.float32, low / len(shards), largest / len(shards))
        gain = gain * jnp.repeat(jnp.exp(heights), extent[axis_at] // parts).reshape((-1,) + (1,) * (len(extent) - 1 - axis_at))
    return gain


def normal_values(stream_key, dims, deviation, bound, shards=(), held_as=jnp.bfloat16):
    gain = steps_of(stream_key, dims, shards, -0.22, 0.18) if shards else 1.0
    array = jax.random.normal(stream_key, dims, jnp.float32) * deviation * gain
    return jnp.minimum(jnp.maximum(array, -bound), bound).astype(held_as)


def setup_inputs(seed: int = 0) -> dict:
    arg_keys = jax.random.split(jax.random.key(seed), 5)
    return {
        "data": normal_values(arg_keys[0], (BEAMS, NCHAN, T_TOTAL), 1.0, 6.0, ((1, 64), (2, 8))),
        "delays": draw_delays(jax.random.fold_in(arg_keys[4], 71), 0),
        "offsets": draw_offsets(jax.random.fold_in(arg_keys[4], 71), 0),
        "widths": draw_widths(jax.random.fold_in(arg_keys[4], 71), 0),
    }


def reference(data, delays, offsets, widths):
    beams, chans, total = data.shape
    nsub = offsets.shape[1]
    per_sub = chans // nsub
    span = total + OMAX
    padded = jnp.pad(data.astype(jnp.float32), ((0, 0), (0, 0), (0, OMAX + DCH - 1)))
    shifted = jnp.zeros((beams, chans, span), jnp.float32)
    for delay in range(DCH):
        shifted = shifted + jnp.where((delays == delay)[None, :, None], padded[:, :, delay:delay + span], 0.0)
    series = shifted.reshape(beams, nsub, per_sub, span).sum(axis=2).astype(jnp.bfloat16)
    times = jnp.arange(total, dtype=jnp.int32)

    def accumulate(running, inputs):
        series_row, lags = inputs
        picked = series_row[:, times[None, :] + lags[:, None]]
        return (running + picked.astype(jnp.float32), None)
    initial_prefix_sums = jnp.zeros((beams, NDM, total), jnp.float32)
    sums, unused = lax.scan(accumulate, initial_prefix_sums, (jnp.transpose(series, (1, 0, 2)), jnp.transpose(offsets)))
    scale = 1.0 / math.sqrt(chans)
    dedispersed = (sums * scale).astype(jnp.bfloat16)
    cumulative_total = jnp.cumsum(dedispersed.astype(jnp.float32), axis=2)
    cumulative_total = jnp.concatenate([jnp.zeros((beams, NDM, 1), jnp.float32), cumulative_total], axis=2)
    cumulative_total = jnp.pad(cumulative_total, ((0, 0), (0, 0), (0, WMAX - 1)), mode='edge')
    lower = cumulative_total[:, :, :total]
    filtered = []
    for column in range(NW):
        width = widths[column].astype(jnp.int32)
        upper = lax.dynamic_slice_in_dim(cumulative_total, width, total, 2)
        filtered.append((upper - lower) / jnp.sqrt(width.astype(jnp.float32)))
    stacked = jnp.stack(filtered, axis=0)
    return jnp.transpose(stacked, (2, 1, 0, 3))
```

```python
import functools
import math

import jax
import jax.numpy as jnp
from jax import lax
from jax.experimental import pallas as pl
from jax.experimental.pallas import tpu as pltpu
from jax.sharding import PartitionSpec as P

WMAX = 128
DCH = 16
OMAX = 96
RING = 8
LANES = 128
EDGE = 112
STEP = 8
MESH = pl.DeviceIdType.MESH
FAR_FIRST = (4, 3, 5, 2, 6, 1, 7)
NEAR_FIRST = (1, 7, 2, 6, 3, 5, 4)


def iota(shape, dim):
    return lax.broadcasted_iota(jnp.int32, shape, dim)


def dedisperse_kernel(
    scale,
    blocks,
    data_ref,
    delays_ref,
    offsets_ref,
    out_ref,
    lag_out,
    lags,
    own_buf,
    halo_out,
    halo_buf,
    series_buf,
    part_buf,
    sum_buf,
    send_own,
    recv_own,
    send_halo,
    recv_halo,
    send_lag,
    recv_lag,
    send_part,
    recv_part,
    send_edge,
    recv_edge,
):
    sub = lax.axis_index("sub")
    tm = lax.axis_index("tm")
    z, y = sub // RING, sub % RING
    chans, length = data_ref.shape
    per = own_buf.shape[1]
    dms = lag_out.shape[1]
    first, last = tm == 0, tm == blocks - 1

    def along_y(d):
        return z * RING + lax.rem(y + d, RING)

    def along_z(d):
        return lax.rem(z + d, RING) * RING + y

    barrier = pltpu.get_barrier_semaphore()

    def greet(block, with_self):
        for d in range(0 if with_self else 1, RING):
            pl.semaphore_signal(barrier, inc=1, device_id=(along_y(d), block), device_id_type=MESH)
        for d in range(1, RING):
            pl.semaphore_signal(barrier, inc=1, device_id=(along_z(d), block), device_id_type=MESH)

    greet(tm, False)

    @pl.when(tm > 0)
    def _():
        greet(tm - 1, True)

    @pl.when(tm < blocks - 1)
    def _():
        greet(tm + 1, True)

    for g in range(RING):
        lag_out[g] = offsets_ref[:, g * LANES : (g + 1) * LANES].astype(jnp.float32).astype(jnp.bfloat16)
    lags[z] = lag_out[z]

    eye = iota((chans, chans), 0) == iota((chans, chans), 1)
    diagonal = jnp.where(eye, delays_ref[...], 0).astype(jnp.float32).astype(jnp.bfloat16)
    delay = jnp.dot(diagonal, jnp.ones((chans, LANES), jnp.bfloat16), preferred_element_type=jnp.float32)
    delay = delay.astype(jnp.int32)
    delay = jnp.concatenate([delay] * 3, axis=1)
    wide = length + LANES
    moved = jnp.concatenate(
        [jnp.zeros((chans, LANES), jnp.float32), data_ref[...].astype(jnp.float32)], axis=1
    )
    for bit in (1, 2, 4, 8):
        moved = jnp.where((delay & bit) != 0, pltpu.roll(moved, wide - bit, 1), moved)
    member = (iota((per, chans), 1) // (chans // per) == iota((per, chans), 0)).astype(jnp.float32)
    summed = jnp.dot(
        member.astype(jnp.bfloat16), moved.astype(jnp.bfloat16), preferred_element_type=jnp.float32
    )
    own_buf[y] = summed[:, LANES:].astype(jnp.bfloat16)
    halo_out[...] = jnp.where(
        iota((per, LANES), 1) < EDGE, summed[:, LANES : 2 * LANES], summed[:, :LANES]
    ).astype(jnp.bfloat16)

    pl.semaphore_wait(
        barrier,
        2 * (RING - 1)
        + (2 * RING - 1) * (jnp.where(first, 0, 1) + jnp.where(last, 0, 1)),
    )

    def lag_copy(d, source):
        g = lax.rem(z + d, RING)
        return pltpu.make_async_remote_copy(
            src_ref=lag_out.at[g],
            dst_ref=lags.at[source],
            send_sem=send_lag.at[d],
            recv_sem=recv_lag.at[source],
            device_id=(along_z(d), tm),
            device_id_type=MESH,
        )

    def own_copy(d, source):
        return pltpu.make_async_remote_copy(
            src_ref=own_buf.at[y],
            dst_ref=own_buf.at[source],
            send_sem=send_own.at[d],
            recv_sem=recv_own.at[source],
            device_id=(along_y(d), tm),
            device_id_type=MESH,
        )

    def halo_copy(d, source):
        return pltpu.make_async_remote_copy(
            src_ref=halo_out,
            dst_ref=halo_buf.at[source],
            send_sem=send_halo.at[d],
            recv_sem=recv_halo.at[source],
            device_id=(along_y(d), tm - 1),
            device_id_type=MESH,
        )

    for d in FAR_FIRST:
        own_copy(d, y).start()
        lag_copy(d, z).start()

    @pl.when(tm > 0)
    def _():
        for d in FAR_FIRST + (0,):
            halo_copy(d, y).start()

    @pl.when(last)
    def _():
        halo_buf[...] = jnp.zeros(halo_buf.shape, halo_buf.dtype)

    for d in NEAR_FIRST:
        lag_copy(d, lax.rem(z + d, RING)).wait_recv()
        own_copy(d, lax.rem(y + d, RING)).wait_recv()

    @pl.when(jnp.logical_not(last))
    def _():
        for d in (0,) + NEAR_FIRST:
            halo_copy(d, lax.rem(y + d, RING)).wait_recv()

    rows = RING * per
    own = own_buf[...].reshape(rows, length)
    halo = halo_buf[...].reshape(rows, LANES)
    edge = jnp.where(iota((rows, LANES), 1) >= EDGE, halo.astype(jnp.float32), 0.0)
    tail = (own[:, length - LANES :].astype(jnp.float32) + edge).astype(jnp.bfloat16)
    series_buf[...] = jnp.concatenate([own[:, : length - LANES], tail, halo], axis=1)

    table = lags[...].reshape(RING * dms, rows)

    def some_lags(block, total):
        base = block * STEP
        here = pltpu.roll(series_buf[...], wide - base, 1)
        masks, windows = [], []
        for j in range(STEP):
            lag = (base + j).astype(jnp.float32).astype(jnp.bfloat16)
            masks.append(jnp.where(table == lag, jnp.bfloat16(1), jnp.bfloat16(0)))
            windows.append(here[:, j : j + length])
        return total + jnp.dot(
            jnp.concatenate(masks, axis=1),
            jnp.concatenate(windows, axis=0),
            preferred_element_type=jnp.float32,
        )

    total = lax.fori_loop(
        0, pl.cdiv(OMAX + 1, STEP), some_lags, jnp.zeros((RING * dms, length), jnp.float32)
    )
    part_buf[...] = total.astype(jnp.bfloat16).reshape(RING, dms, length)

    def part_copy(d, source):
        g = lax.rem(z + d, RING)
        return pltpu.make_async_remote_copy(
            src_ref=part_buf.at[g],
            dst_ref=sum_buf.at[source, :, pl.ds(0, length)],
            send_sem=send_part.at[d],
            recv_sem=recv_part.at[source],
            device_id=(along_z(d), tm),
            device_id_type=MESH,
        )

    def edge_copy(d, source):
        g = lax.rem(z + d, RING)
        return pltpu.make_async_remote_copy(
            src_ref=part_buf.at[g, :, pl.ds(0, LANES)],
            dst_ref=sum_buf.at[source, :, pl.ds(length, LANES)],
            send_sem=send_edge.at[d],
            recv_sem=recv_edge.at[source],
            device_id=(along_z(d), tm - 1),
            device_id_type=MESH,
        )

    for d in FAR_FIRST:
        part_copy(d, z).start()

    @pl.when(tm > 0)
    def _():
        for d in FAR_FIRST + (0,):
            edge_copy(d, z).start()

    @pl.when(last)
    def _():
        sum_buf[:, :, length:] = jnp.zeros((RING, dms, LANES), jnp.bfloat16)

    sum_buf[z, :, :length] = part_buf[z]

    for d in NEAR_FIRST:
        part_copy(d, lax.rem(z + d, RING)).wait_recv()

    @pl.when(jnp.logical_not(last))
    def _():
        for d in (0,) + NEAR_FIRST:
            edge_copy(d, lax.rem(z + d, RING)).wait_recv()

    added = sum_buf[0].astype(jnp.float32)
    for g in range(1, RING):
        added = added + sum_buf[g].astype(jnp.float32)
    out_ref[...] = (added * scale).astype(jnp.bfloat16)

    for d in NEAR_FIRST:
        own_copy(d, y).wait_send()
        lag_copy(d, z).wait_send()
        part_copy(d, z).wait_send()

    @pl.when(tm > 0)
    def _():
        for d in (0,) + NEAR_FIRST:
            halo_copy(d, y).wait_send()
            edge_copy(d, z).wait_send()


def boxcar_kernel(widths_ref, series_ref, out_ref, woven):
    span = series_ref.shape[1]
    length = out_ref.shape[1]
    count = widths_ref.shape[0]
    dms = series_ref.shape[0]
    lag = iota((span, length), 0) - iota((span, length), 1)
    for i in range(count):
        width = widths_ref[i]
        window = jnp.where((lag >= 0) & (lag < width), 1.0, 0.0).astype(jnp.bfloat16)
        total = jnp.dot(series_ref[...], window, preferred_element_type=jnp.float32)
        root = jnp.sqrt(jnp.full((dms, length), width, jnp.int32).astype(jnp.float32))
        total = total / root
        for h in range(length // LANES):
            woven[h, pl.ds(i, dms, stride=count), :] = total[:, h * LANES : (h + 1) * LANES]
    for h in range(length // LANES):
        out_ref[:, h * LANES : (h + 1) * LANES] = woven[h]


def solution(mesh):
    blocks = mesh.shape["tm"]

    def per_device(data, delays, offsets, widths):
        _, chans, length = data.shape
        dms, nsub = offsets.shape
        groups = lax.axis_size("sub")
        per = nsub // groups
        scale = 1.0 / math.sqrt(chans * groups)
        vmem = pl.BlockSpec(memory_space=pltpu.VMEM)
        bf16 = jnp.bfloat16
        dma = pltpu.SemaphoreType.DMA((RING,))
        series = pl.pallas_call(
            functools.partial(dedisperse_kernel, scale, blocks),
            out_shape=jax.ShapeDtypeStruct((dms, length + LANES), bf16),
            in_specs=[vmem] * 3,
            out_specs=vmem,
            scratch_shapes=[
                pltpu.VMEM((RING, dms, LANES), bf16),
                pltpu.VMEM((RING, dms, LANES), bf16),
                pltpu.VMEM((RING, per, length), bf16),
                pltpu.VMEM((per, LANES), bf16),
                pltpu.VMEM((RING, per, LANES), bf16),
                pltpu.VMEM((RING * per, length + LANES), bf16),
                pltpu.VMEM((RING, dms, length), bf16),
                pltpu.VMEM((RING, dms, length + LANES), bf16),
            ]
            + [dma] * 10,
            compiler_params=pltpu.CompilerParams(collective_id=0, has_side_effects=True),
        )(data[0], delays[None, :], offsets)
        count = widths.shape[0]
        out = pl.pallas_call(
            boxcar_kernel,
            out_shape=jax.ShapeDtypeStruct((dms * count, length), jnp.float32),
            in_specs=[pl.BlockSpec(memory_space=pltpu.SMEM), vmem],
            out_specs=vmem,
            scratch_shapes=[pltpu.VMEM((length // LANES, dms * count, LANES), jnp.float32)],
        )(widths, series)
        return out.reshape(dms, 1, count, length)

    placed = (P(None, "sub", "tm"), P("sub"), P("sub", None), P())
    return jax.shard_map(
        per_device,
        mesh=mesh,
        in_specs=placed,
        out_specs=P("sub", None, None, "tm"),
        check_vma=False,
    )
```

```python
import functools
import math

import jax
import jax.numpy as jnp
from jax import lax
from jax.experimental import pallas as pl
from jax.experimental.pallas import tpu as pltpu
from jax.sharding import PartitionSpec as P

WMAX = 128
DCH = 16
OMAX = 96
RING = 8
LANES = 128
EDGE = 112
STEP = 97
MESH = pl.DeviceIdType.MESH
FAR_FIRST = (4, 3, 5, 2, 6, 1, 7)
NEAR_FIRST = (1, 7, 2, 6, 3, 5, 4)


def iota(shape, dim):
    return lax.broadcasted_iota(jnp.int32, shape, dim)


def dedisperse_kernel(
    scale,
    blocks,
    data_ref,
    delays_ref,
    offsets_ref,
    out_ref,
    lag_out,
    lags,
    own_buf,
    halo_out,
    halo_buf,
    turned,
    part_buf,
    sum_buf,
    send_own,
    recv_own,
    send_halo,
    recv_halo,
    send_lag,
    recv_lag,
    send_part,
    recv_part,
    send_edge,
    recv_edge,
):
    sub = lax.axis_index("sub")
    tm = lax.axis_index("tm")
    z, y = sub // RING, sub % RING
    chans, length = data_ref.shape
    per = own_buf.shape[1]
    dms = lag_out.shape[1]
    first, last = tm == 0, tm == blocks - 1

    def along_y(d):
        return z * RING + lax.rem(y + d, RING)

    def along_z(d):
        return lax.rem(z + d, RING) * RING + y

    barrier = pltpu.get_barrier_semaphore()

    def greet(block, with_self):
        for d in range(0 if with_self else 1, RING):
            pl.semaphore_signal(barrier, inc=1, device_id=(along_y(d), block), device_id_type=MESH)
        for d in range(1, RING):
            pl.semaphore_signal(barrier, inc=1, device_id=(along_z(d), block), device_id_type=MESH)

    greet(tm, False)

    @pl.when(tm > 0)
    def _():
        greet(tm - 1, True)

    @pl.when(tm < blocks - 1)
    def _():
        greet(tm + 1, True)

    for g in range(RING):
        lag_out[g] = offsets_ref[:, g * LANES : (g + 1) * LANES].astype(jnp.float32).astype(jnp.bfloat16)
    lags[z] = lag_out[z]

    eye = iota((chans, chans), 0) == iota((chans, chans), 1)
    diagonal = jnp.where(eye, delays_ref[...], 0).astype(jnp.float32).astype(jnp.bfloat16)
    delay = jnp.dot(diagonal, jnp.ones((chans, LANES), jnp.bfloat16), preferred_element_type=jnp.float32)
    delay = delay.astype(jnp.int32)
    delay = jnp.concatenate([delay] * 3, axis=1)
    wide = length + LANES
    moved = jnp.concatenate(
        [jnp.zeros((chans, LANES), jnp.float32), data_ref[...].astype(jnp.float32)], axis=1
    )
    for bit in (1, 2, 4, 8):
        moved = jnp.where((delay & bit) != 0, pltpu.roll(moved, wide - bit, 1), moved)
    member = (iota((per, chans), 1) // (chans // per) == iota((per, chans), 0)).astype(jnp.float32)
    summed = jnp.dot(
        member.astype(jnp.bfloat16), moved.astype(jnp.bfloat16), preferred_element_type=jnp.float32
    )
    own_buf[y] = summed[:, LANES:].astype(jnp.bfloat16)
    halo_out[...] = jnp.where(
        iota((per, LANES), 1) < EDGE, summed[:, LANES : 2 * LANES], summed[:, :LANES]
    ).astype(jnp.bfloat16)

    pl.semaphore_wait(
        barrier,
        2 * (RING - 1)
        + (2 * RING - 1) * (jnp.where(first, 0, 1) + jnp.where(last, 0, 1)),
    )

    def lag_copy(d, source):
        g = lax.rem(z + d, RING)
        return pltpu.make_async_remote_copy(
            src_ref=lag_out.at[g],
            dst_ref=lags.at[source],
            send_sem=send_lag.at[d],
            recv_sem=recv_lag.at[source],
            device_id=(along_z(d), tm),
            device_id_type=MESH,
        )

    def own_copy(d, source):
        return pltpu.make_async_remote_copy(
            src_ref=own_buf.at[y],
            dst_ref=own_buf.at[source],
            send_sem=send_own.at[d],
            recv_sem=recv_own.at[source],
            device_id=(along_y(d), tm),
            device_id_type=MESH,
        )

    def halo_copy(d, source):
        return pltpu.make_async_remote_copy(
            src_ref=halo_out,
            dst_ref=halo_buf.at[source],
            send_sem=send_halo.at[d],
            recv_sem=recv_halo.at[source],
            device_id=(along_y(d), tm - 1),
            device_id_type=MESH,
        )

    for d in FAR_FIRST:
        own_copy(d, y).start()
        lag_copy(d, z).start()

    @pl.when(tm > 0)
    def _():
        for d in FAR_FIRST + (0,):
            halo_copy(d, y).start()

    @pl.when(last)
    def _():
        halo_buf[...] = jnp.zeros(halo_buf.shape, halo_buf.dtype)

    for d in NEAR_FIRST:
        lag_copy(d, lax.rem(z + d, RING)).wait_recv()
        own_copy(d, lax.rem(y + d, RING)).wait_recv()

    @pl.when(jnp.logical_not(last))
    def _():
        for d in (0,) + NEAR_FIRST:
            halo_copy(d, lax.rem(y + d, RING)).wait_recv()

    rows = RING * per
    own = own_buf[...].reshape(rows, length)
    halo = halo_buf[...].reshape(rows, LANES)
    edge = jnp.where(iota((rows, LANES), 1) >= EDGE, halo.astype(jnp.float32), 0.0)
    tail = own[:, length - LANES :].astype(jnp.float32) + edge
    tail = tail.astype(jnp.bfloat16).astype(jnp.float32)
    body = own[:, : length - LANES].astype(jnp.float32)
    turned[...] = jnp.concatenate([body, tail, halo.astype(jnp.float32)], axis=1).T

    table = lags[...].reshape(RING * dms, rows).astype(jnp.float32).T.astype(jnp.bfloat16)

    def some_lags(block, total):
        base = block * STEP
        masks, windows = [], []
        for j in range(STEP):
            lag = (base + j).astype(jnp.float32).astype(jnp.bfloat16)
            masks.append(jnp.where(table == lag, jnp.bfloat16(1), jnp.bfloat16(0)))
            windows.append(turned[pl.ds(base + j, length), :].astype(jnp.bfloat16))
        return total + jnp.dot(
            jnp.concatenate(windows, axis=1),
            jnp.concatenate(masks, axis=0),
            preferred_element_type=jnp.float32,
        )

    total = lax.fori_loop(
        0, pl.cdiv(OMAX + 1, STEP), some_lags, jnp.zeros((length, RING * dms), jnp.float32)
    )
    part_buf[...] = total.T.astype(jnp.bfloat16).reshape(RING, dms, length)

    def part_copy(d, source):
        g = lax.rem(z + d, RING)
        return pltpu.make_async_remote_copy(
            src_ref=part_buf.at[g],
            dst_ref=sum_buf.at[source, :, pl.ds(0, length)],
            send_sem=send_part.at[d],
            recv_sem=recv_part.at[source],
            device_id=(along_z(d), tm),
            device_id_type=MESH,
        )

    def edge_copy(d, source):
        g = lax.rem(z + d, RING)
        return pltpu.make_async_remote_copy(
            src_ref=part_buf.at[g, :, pl.ds(0, LANES)],
            dst_ref=sum_buf.at[source, :, pl.ds(length, LANES)],
            send_sem=send_edge.at[d],
            recv_sem=recv_edge.at[source],
            device_id=(along_z(d), tm - 1),
            device_id_type=MESH,
        )

    for d in FAR_FIRST:
        part_copy(d, z).start()

    @pl.when(tm > 0)
    def _():
        for d in FAR_FIRST + (0,):
            edge_copy(d, z).start()

    @pl.when(last)
    def _():
        sum_buf[:, :, length:] = jnp.zeros((RING, dms, LANES), jnp.bfloat16)

    sum_buf[z, :, :length] = part_buf[z]

    for d in NEAR_FIRST:
        part_copy(d, lax.rem(z + d, RING)).wait_recv()

    @pl.when(jnp.logical_not(last))
    def _():
        for d in (0,) + NEAR_FIRST:
            edge_copy(d, lax.rem(z + d, RING)).wait_recv()

    added = sum_buf[0].astype(jnp.float32)
    for g in range(1, RING):
        added = added + sum_buf[g].astype(jnp.float32)
    out_ref[...] = (added * scale).astype(jnp.bfloat16)

    for d in NEAR_FIRST:
        own_copy(d, y).wait_send()
        lag_copy(d, z).wait_send()
        part_copy(d, z).wait_send()

    @pl.when(tm > 0)
    def _():
        for d in (0,) + NEAR_FIRST:
            halo_copy(d, y).wait_send()
            edge_copy(d, z).wait_send()


def boxcar_kernel(widths_ref, series_ref, out_ref, woven):
    span = series_ref.shape[1]
    length = out_ref.shape[1]
    count = widths_ref.shape[0]
    dms = series_ref.shape[0]
    lag = iota((span, length), 0) - iota((span, length), 1)
    for i in range(count):
        width = widths_ref[i]
        window = jnp.where((lag >= 0) & (lag < width), 1.0, 0.0).astype(jnp.bfloat16)
        total = jnp.dot(series_ref[...], window, preferred_element_type=jnp.float32)
        root = jnp.sqrt(jnp.full((dms, length), width, jnp.int32).astype(jnp.float32))
        total = total / root
        for h in range(length // LANES):
            woven[h, pl.ds(i, dms, stride=count), :] = total[:, h * LANES : (h + 1) * LANES]
    for h in range(length // LANES):
        out_ref[:, h * LANES : (h + 1) * LANES] = woven[h]


def solution(mesh):
    blocks = mesh.shape["tm"]

    def per_device(data, delays, offsets, widths):
        _, chans, length = data.shape
        dms, nsub = offsets.shape
        groups = lax.axis_size("sub")
        per = nsub // groups
        scale = 1.0 / math.sqrt(chans * groups)
        vmem = pl.BlockSpec(memory_space=pltpu.VMEM)
        bf16 = jnp.bfloat16
        dma = pltpu.SemaphoreType.DMA((RING,))
        series = pl.pallas_call(
            functools.partial(dedisperse_kernel, scale, blocks),
            out_shape=jax.ShapeDtypeStruct((dms, length + LANES), bf16),
            in_specs=[vmem] * 3,
            out_specs=vmem,
            scratch_shapes=[
                pltpu.VMEM((RING, dms, LANES), bf16),
                pltpu.VMEM((RING, dms, LANES), bf16),
                pltpu.VMEM((RING, per, length), bf16),
                pltpu.VMEM((per, LANES), bf16),
                pltpu.VMEM((RING, per, LANES), bf16),
                pltpu.VMEM((length + LANES, RING * per), jnp.float32),
                pltpu.VMEM((RING, dms, length), bf16),
                pltpu.VMEM((RING, dms, length + LANES), bf16),
            ]
            + [dma] * 10,
            compiler_params=pltpu.CompilerParams(collective_id=0, has_side_effects=True),
        )(data[0], delays[None, :], offsets)
        count = widths.shape[0]
        out = pl.pallas_call(
            boxcar_kernel,
            out_shape=jax.ShapeDtypeStruct((dms * count, length), jnp.float32),
            in_specs=[pl.BlockSpec(memory_space=pltpu.SMEM), vmem],
            out_specs=vmem,
            scratch_shapes=[pltpu.VMEM((length // LANES, dms * count, LANES), jnp.float32)],
        )(widths, series)
        return out.reshape(dms, 1, count, length)

    placed = (P(None, "sub", "tm"), P("sub"), P("sub", None), P())
    return jax.shard_map(
        per_device,
        mesh=mesh,
        in_specs=placed,
        out_specs=P("sub", None, None, "tm"),
        check_vma=False,
    )
```

```python
import functools
import math

import jax
import jax.numpy as jnp
from jax import lax
from jax.experimental import pallas as pl
from jax.experimental.pallas import tpu as pltpu
from jax.sharding import PartitionSpec as P

WMAX = 128
DCH = 16
OMAX = 96
RING = 8
LANES = 128
EDGE = 112
STEP = 97
MESH = pl.DeviceIdType.MESH
FAR_FIRST = (4, 3, 5, 2, 6, 1, 7)
NEAR_FIRST = (1, 7, 2, 6, 3, 5, 4)


def iota(shape, dim):
    return lax.broadcasted_iota(jnp.int32, shape, dim)


def dedisperse_kernel(
    scale,
    blocks,
    data_hbm,
    delays_hbm,
    offsets_hbm,
    out_ref,
    data_ref,
    delays_ref,
    offsets_ref,
    lag_out,
    lags,
    own_buf,
    halo_out,
    halo_buf,
    turned,
    part_buf,
    sum_buf,
    send_own,
    recv_own,
    send_halo,
    recv_halo,
    send_lag,
    recv_lag,
    send_part,
    recv_part,
    send_edge,
    recv_edge,
    load,
):
    sub = lax.axis_index("sub")
    tm = lax.axis_index("tm")
    z, y = sub // RING, sub % RING
    chans, length = data_ref.shape
    per = own_buf.shape[1]
    dms = lag_out.shape[1]
    first, last = tm == 0, tm == blocks - 1

    def along_y(d):
        return z * RING + lax.rem(y + d, RING)

    def along_z(d):
        return lax.rem(z + d, RING) * RING + y

    barrier = pltpu.get_barrier_semaphore()

    def fetch(i, source, target):
        return pltpu.make_async_copy(source, target, load.at[i])

    fetch(0, data_hbm, data_ref).start()
    fetch(1, delays_hbm, delays_ref).start()
    fetch(2, offsets_hbm, offsets_ref).start()

    def greet(block, with_self):
        for d in FAR_FIRST:
            pl.semaphore_signal(barrier, inc=1, device_id=(along_y(d), block), device_id_type=MESH)
            pl.semaphore_signal(barrier, inc=1, device_id=(along_z(d), block), device_id_type=MESH)
        if with_self:
            pl.semaphore_signal(barrier, inc=1, device_id=(along_y(0), block), device_id_type=MESH)

    greet(tm, False)

    @pl.when(tm < blocks - 1)
    def _():
        greet(tm + 1, True)

    fetch(2, offsets_hbm, offsets_ref).wait()
    for g in range(RING):
        lag_out[g] = offsets_ref[:, g * LANES : (g + 1) * LANES].astype(jnp.float32).astype(jnp.bfloat16)
    lags[z] = lag_out[z]

    fetch(0, data_hbm, data_ref).wait()
    fetch(1, delays_hbm, delays_ref).wait()
    eye = iota((chans, chans), 0) == iota((chans, chans), 1)
    diagonal = jnp.where(eye, delays_ref[...], 0).astype(jnp.float32).astype(jnp.bfloat16)
    delay = jnp.dot(diagonal, jnp.ones((chans, LANES), jnp.bfloat16), preferred_element_type=jnp.float32)
    delay = delay.astype(jnp.int32)
    delay = jnp.concatenate([delay] * 3, axis=1)
    wide = length + LANES
    moved = jnp.concatenate(
        [jnp.zeros((chans, LANES), jnp.float32), data_ref[...].astype(jnp.float32)], axis=1
    )
    for bit in (1, 2, 4, 8):
        moved = jnp.where((delay & bit) != 0, pltpu.roll(moved, wide - bit, 1), moved)
    member = (iota((per, chans), 1) // (chans // per) == iota((per, chans), 0)).astype(jnp.float32)
    summed = jnp.dot(
        member.astype(jnp.bfloat16), moved.astype(jnp.bfloat16), preferred_element_type=jnp.float32
    )
    own_buf[y] = summed[:, LANES:].astype(jnp.bfloat16)
    halo_out[...] = jnp.where(
        iota((per, LANES), 1) < EDGE, summed[:, LANES : 2 * LANES], summed[:, :LANES]
    ).astype(jnp.bfloat16)

    pl.semaphore_wait(
        barrier,
        2 * (RING - 1) + jnp.where(first, 0, 2 * RING - 1),
    )

    def lag_copy(d, source):
        g = lax.rem(z + d, RING)
        return pltpu.make_async_remote_copy(
            src_ref=lag_out.at[g],
            dst_ref=lags.at[source],
            send_sem=send_lag.at[d],
            recv_sem=recv_lag.at[source],
            device_id=(along_z(d), tm),
            device_id_type=MESH,
        )

    def own_copy(d, source):
        return pltpu.make_async_remote_copy(
            src_ref=own_buf.at[y],
            dst_ref=own_buf.at[source],
            send_sem=send_own.at[d],
            recv_sem=recv_own.at[source],
            device_id=(along_y(d), tm),
            device_id_type=MESH,
        )

    def halo_copy(d, source):
        return pltpu.make_async_remote_copy(
            src_ref=halo_out,
            dst_ref=halo_buf.at[source],
            send_sem=send_halo.at[d],
            recv_sem=recv_halo.at[source],
            device_id=(along_y(d), tm - 1),
            device_id_type=MESH,
        )

    for d in FAR_FIRST:
        own_copy(d, y).start()
        lag_copy(d, z).start()

    @pl.when(tm > 0)
    def _():
        for d in FAR_FIRST + (0,):
            halo_copy(d, y).start()

    @pl.when(last)
    def _():
        halo_buf[...] = jnp.zeros(halo_buf.shape, halo_buf.dtype)

    for d in NEAR_FIRST:
        lag_copy(d, lax.rem(z + d, RING)).wait_recv()
        own_copy(d, lax.rem(y + d, RING)).wait_recv()

    @pl.when(jnp.logical_not(last))
    def _():
        for d in (0,) + NEAR_FIRST:
            halo_copy(d, lax.rem(y + d, RING)).wait_recv()

    rows = RING * per
    own = own_buf[...].reshape(rows, length)
    halo = halo_buf[...].reshape(rows, LANES)
    edge = jnp.where(iota((rows, LANES), 1) >= EDGE, halo.astype(jnp.float32), 0.0)
    tail = own[:, length - LANES :].astype(jnp.float32) + edge
    tail = tail.astype(jnp.bfloat16).astype(jnp.float32)
    body = own[:, : length - LANES].astype(jnp.float32)
    turned[...] = jnp.concatenate([body, tail, halo.astype(jnp.float32)], axis=1).T

    table = lags[...].reshape(RING * dms, rows).astype(jnp.float32).T.astype(jnp.bfloat16)

    def some_lags(block, total):
        base = block * STEP
        masks, windows = [], []
        for j in range(STEP):
            lag = (base + j).astype(jnp.float32).astype(jnp.bfloat16)
            masks.append(jnp.where(table == lag, jnp.bfloat16(1), jnp.bfloat16(0)))
            windows.append(turned[pl.ds(base + j, length), :].astype(jnp.bfloat16))
        return total + jnp.dot(
            jnp.concatenate(windows, axis=1),
            jnp.concatenate(masks, axis=0),
            preferred_element_type=jnp.float32,
        )

    total = lax.fori_loop(
        0, pl.cdiv(OMAX + 1, STEP), some_lags, jnp.zeros((length, RING * dms), jnp.float32)
    )
    part_buf[...] = total.T.astype(jnp.bfloat16).reshape(RING, dms, length)

    def part_copy(d, source):
        g = lax.rem(z + d, RING)
        return pltpu.make_async_remote_copy(
            src_ref=part_buf.at[g],
            dst_ref=sum_buf.at[source, :, pl.ds(0, length)],
            send_sem=send_part.at[d],
            recv_sem=recv_part.at[source],
            device_id=(along_z(d), tm),
            device_id_type=MESH,
        )

    def edge_copy(d, source):
        g = lax.rem(z + d, RING)
        return pltpu.make_async_remote_copy(
            src_ref=part_buf.at[g, :, pl.ds(0, LANES)],
            dst_ref=sum_buf.at[source, :, pl.ds(length, LANES)],
            send_sem=send_edge.at[d],
            recv_sem=recv_edge.at[source],
            device_id=(along_z(d), tm - 1),
            device_id_type=MESH,
        )

    for d in FAR_FIRST:
        part_copy(d, z).start()

    @pl.when(tm > 0)
    def _():
        for d in FAR_FIRST + (0,):
            edge_copy(d, z).start()

    @pl.when(last)
    def _():
        sum_buf[:, :, length:] = jnp.zeros((RING, dms, LANES), jnp.bfloat16)

    sum_buf[z, :, :length] = part_buf[z]

    for d in NEAR_FIRST:
        part_copy(d, lax.rem(z + d, RING)).wait_recv()

    @pl.when(jnp.logical_not(last))
    def _():
        for d in (0,) + NEAR_FIRST:
            edge_copy(d, lax.rem(z + d, RING)).wait_recv()

    added = sum_buf[0].astype(jnp.float32)
    for g in range(1, RING):
        added = added + sum_buf[g].astype(jnp.float32)
    out_ref[...] = (added * scale).astype(jnp.bfloat16)

    for d in NEAR_FIRST:
        own_copy(d, y).wait_send()
        lag_copy(d, z).wait_send()
        part_copy(d, z).wait_send()

    @pl.when(tm > 0)
    def _():
        for d in (0,) + NEAR_FIRST:
            halo_copy(d, y).wait_send()
            edge_copy(d, z).wait_send()


def boxcar_kernel(widths_ref, series_ref, out_ref, woven):
    length = out_ref.shape[1]
    count = widths_ref.shape[0]
    dms = series_ref.shape[0]
    tiles = length // LANES
    spans = [series_ref[:, h * LANES : (h + 2) * LANES] for h in range(tiles)]
    spans = jnp.concatenate(spans, axis=0)
    lag = iota((2 * LANES, LANES), 0) - iota((2 * LANES, LANES), 1)
    lag = jnp.where(lag < 0, WMAX, lag)
    for i in range(count):
        width = widths_ref[i]
        window = jnp.where(lag < width, 1.0, 0.0).astype(jnp.bfloat16)
        total = jnp.dot(spans, window, preferred_element_type=jnp.float32)
        total = total / jnp.sqrt(jnp.full((1, LANES), width, jnp.int32).astype(jnp.float32))
        for h in range(tiles):
            woven[h, pl.ds(i, dms, stride=count), :] = total[h * dms : (h + 1) * dms]
    for h in range(tiles):
        out_ref[:, h * LANES : (h + 1) * LANES] = woven[h]


def solution(mesh):
    blocks = mesh.shape["tm"]

    def per_device(data, delays, offsets, widths):
        _, chans, length = data.shape
        dms, nsub = offsets.shape
        groups = lax.axis_size("sub")
        per = nsub // groups
        scale = 1.0 / math.sqrt(chans * groups)
        vmem = pl.BlockSpec(memory_space=pltpu.VMEM)
        bf16 = jnp.bfloat16
        dma = pltpu.SemaphoreType.DMA((RING,))
        series = pl.pallas_call(
            functools.partial(dedisperse_kernel, scale, blocks),
            out_shape=jax.ShapeDtypeStruct((dms, length + LANES), bf16),
            in_specs=[pl.BlockSpec(memory_space=pl.ANY)] * 3,
            out_specs=vmem,
            scratch_shapes=[
                pltpu.VMEM((chans, length), bf16),
                pltpu.VMEM((1, chans), jnp.int32),
                pltpu.VMEM((dms, nsub), jnp.int32),
                pltpu.VMEM((RING, dms, LANES), bf16),
                pltpu.VMEM((RING, dms, LANES), bf16),
                pltpu.VMEM((RING, per, length), bf16),
                pltpu.VMEM((per, LANES), bf16),
                pltpu.VMEM((RING, per, LANES), bf16),
                pltpu.VMEM((length + LANES, RING * per), jnp.float32),
                pltpu.VMEM((RING, dms, length), bf16),
                pltpu.VMEM((RING, dms, length + LANES), bf16),
            ]
            + [dma] * 10
            + [pltpu.SemaphoreType.DMA((3,))],
            compiler_params=pltpu.CompilerParams(collective_id=0, has_side_effects=True),
        )(data[0], delays[None, :], offsets)
        count = widths.shape[0]
        out = pl.pallas_call(
            boxcar_kernel,
            out_shape=jax.ShapeDtypeStruct((dms * count, length), jnp.float32),
            in_specs=[pl.BlockSpec(memory_space=pltpu.SMEM), vmem],
            out_specs=vmem,
            scratch_shapes=[pltpu.VMEM((length // LANES, dms * count, LANES), jnp.float32)],
        )(widths, series)
        return out.reshape(dms, 1, count, length)

    placed = (P(None, "sub", "tm"), P("sub"), P("sub", None), P())
    return jax.shard_map(
        per_device,
        mesh=mesh,
        in_specs=placed,
        out_specs=P("sub", None, None, "tm"),
        check_vma=False,
    )
```

```python
import functools
import math

import jax
import jax.numpy as jnp
from jax import lax
from jax.experimental import pallas as pl
from jax.experimental.pallas import tpu as pltpu
from jax.sharding import PartitionSpec as P

WMAX = 128
DCH = 16
OMAX = 96
RING = 8
LANES = 128
EDGE = 112
MESH = pl.DeviceIdType.MESH
FAR_FIRST = (4, 3, 5, 2, 6, 1, 7)
NEAR_FIRST = (1, 7, 2, 6, 3, 5, 4)


def iota(shape, dim):
    return lax.broadcasted_iota(jnp.int32, shape, dim)


def dedisperse_kernel(
    scale,
    blocks,
    data_hbm,
    delays_hbm,
    offsets_hbm,
    out_ref,
    data_ref,
    delays_ref,
    offsets_ref,
    lag_out,
    lags,
    own_buf,
    halo_out,
    halo_buf,
    turned,
    part_buf,
    sum_buf,
    edge_out,
    edge_in,
    send_own,
    recv_own,
    send_halo,
    recv_halo,
    send_lag,
    recv_lag,
    send_part,
    recv_part,
    send_edge,
    recv_edge,
    load,
):
    sub = lax.axis_index("sub")
    tm = lax.axis_index("tm")
    z, y = sub // RING, sub % RING
    chans, length = data_ref.shape
    per = own_buf.shape[1]
    dms = lag_out.shape[1]
    first, last = tm == 0, tm == blocks - 1

    def along_y(d):
        return z * RING + lax.rem(y + d, RING)

    def along_z(d):
        return lax.rem(z + d, RING) * RING + y

    barrier = pltpu.get_barrier_semaphore()

    def fetch(i, source, target):
        return pltpu.make_async_copy(source, target, load.at[i])

    fetch(0, data_hbm, data_ref).start()
    fetch(1, delays_hbm, delays_ref).start()
    fetch(2, offsets_hbm, offsets_ref).start()

    for d in FAR_FIRST:
        pl.semaphore_signal(barrier, inc=1, device_id=(along_y(d), tm), device_id_type=MESH)
        pl.semaphore_signal(barrier, inc=1, device_id=(along_z(d), tm), device_id_type=MESH)

    @pl.when(jnp.logical_not(last))
    def _():
        for d in FAR_FIRST + (0,):
            pl.semaphore_signal(barrier, inc=1, device_id=(along_y(d), tm + 1), device_id_type=MESH)

    fetch(2, offsets_hbm, offsets_ref).wait()
    for g in range(RING):
        lag_out[g] = offsets_ref[:, g * LANES : (g + 1) * LANES].astype(jnp.float32).astype(jnp.bfloat16)
    lags[z] = lag_out[z]

    fetch(0, data_hbm, data_ref).wait()
    fetch(1, delays_hbm, delays_ref).wait()
    eye = iota((chans, chans), 0) == iota((chans, chans), 1)
    diagonal = jnp.where(eye, delays_ref[...], 0).astype(jnp.float32).astype(jnp.bfloat16)
    delay = jnp.dot(diagonal, jnp.ones((chans, LANES), jnp.bfloat16), preferred_element_type=jnp.float32)
    delay = delay.astype(jnp.int32)
    delay = jnp.concatenate([delay] * 3, axis=1)
    wide = length + LANES
    moved = jnp.concatenate(
        [jnp.zeros((chans, LANES), jnp.float32), data_ref[...].astype(jnp.float32)], axis=1
    )
    for bit in (1, 2, 4, 8):
        moved = jnp.where((delay & bit) != 0, pltpu.roll(moved, wide - bit, 1), moved)
    member = (iota((per, chans), 1) // (chans // per) == iota((per, chans), 0)).astype(jnp.float32)
    summed = jnp.dot(
        member.astype(jnp.bfloat16), moved.astype(jnp.bfloat16), preferred_element_type=jnp.float32
    )
    own_buf[y] = summed[:, LANES:].astype(jnp.bfloat16)
    halo_out[...] = jnp.where(
        iota((per, LANES), 1) < EDGE, summed[:, LANES : 2 * LANES], summed[:, :LANES]
    ).astype(jnp.bfloat16)

    pl.semaphore_wait(
        barrier,
        2 * (RING - 1) + jnp.where(first, 0, RING),
    )

    def lag_copy(d, source):
        g = lax.rem(z + d, RING)
        return pltpu.make_async_remote_copy(
            src_ref=lag_out.at[g],
            dst_ref=lags.at[source],
            send_sem=send_lag.at[d],
            recv_sem=recv_lag.at[source],
            device_id=(along_z(d), tm),
            device_id_type=MESH,
        )

    def own_copy(d, source):
        return pltpu.make_async_remote_copy(
            src_ref=own_buf.at[y],
            dst_ref=own_buf.at[source],
            send_sem=send_own.at[d],
            recv_sem=recv_own.at[source],
            device_id=(along_y(d), tm),
            device_id_type=MESH,
        )

    def halo_copy(d, source):
        return pltpu.make_async_remote_copy(
            src_ref=halo_out,
            dst_ref=halo_buf.at[source],
            send_sem=send_halo.at[d],
            recv_sem=recv_halo.at[source],
            device_id=(along_y(d), tm - 1),
            device_id_type=MESH,
        )

    for d in FAR_FIRST:
        own_copy(d, y).start()
        lag_copy(d, z).start()

    @pl.when(tm > 0)
    def _():
        for d in FAR_FIRST + (0,):
            halo_copy(d, y).start()

    @pl.when(last)
    def _():
        halo_buf[...] = jnp.zeros(halo_buf.shape, halo_buf.dtype)

    for d in NEAR_FIRST:
        lag_copy(d, lax.rem(z + d, RING)).wait_recv()
        own_copy(d, lax.rem(y + d, RING)).wait_recv()

    rows = RING * per
    turned[:length] = own_buf[...].reshape(rows, length).astype(jnp.float32).T

    table = lags[...].reshape(RING * dms, rows).astype(jnp.float32).T.astype(jnp.bfloat16)

    def part_copy(t, d, source):
        return pltpu.make_async_remote_copy(
            src_ref=part_buf.at[t, lax.rem(z + d, RING)],
            dst_ref=sum_buf.at[t, source],
            send_sem=send_part.at[t * RING + d],
            recv_sem=recv_part.at[t * RING + source],
            device_id=(along_z(d), tm),
            device_id_type=MESH,
        )

    def edge_copy():
        return pltpu.make_async_remote_copy(
            src_ref=edge_out,
            dst_ref=edge_in,
            send_sem=send_edge.at[0],
            recv_sem=recv_edge.at[0],
            device_id=(sub, tm - 1),
            device_id_type=MESH,
        )

    def add_halo():
        @pl.when(jnp.logical_not(last))
        def _():
            for d in (0,) + NEAR_FIRST:
                halo_copy(d, lax.rem(y + d, RING)).wait_recv()

        halo = halo_buf[...].reshape(rows, LANES).astype(jnp.float32)
        edge = jnp.where(iota((rows, LANES), 1) >= EDGE, halo, 0.0)
        tail = own_buf[:, :, length - LANES :].reshape(rows, LANES).astype(jnp.float32) + edge
        turned[length - LANES : length] = tail.astype(jnp.bfloat16).astype(jnp.float32).T
        turned[length:] = halo.T

    tiles = length // LANES

    def tile(t, carry):
        pl.when(t == tiles - 1)(add_halo)
        masks, windows = [], []
        for j in range(OMAX + 1):
            masks.append(jnp.where(table == jnp.bfloat16(j), jnp.bfloat16(1), jnp.bfloat16(0)))
            windows.append(turned[pl.ds(t * LANES + j, LANES), :].astype(jnp.bfloat16))
        total = jnp.dot(
            jnp.concatenate(windows, axis=1),
            jnp.concatenate(masks, axis=0),
            preferred_element_type=jnp.float32,
        )
        part_buf[t] = total.T.astype(jnp.bfloat16).reshape(RING, dms, LANES)
        for d in FAR_FIRST:
            part_copy(t, d, z).start()

        sum_buf[t, z] = part_buf[t, z]
        return carry

    lax.fori_loop(0, tiles, tile, 0)

    def finish(t):
        for d in NEAR_FIRST:
            part_copy(t, d, lax.rem(z + d, RING)).wait_recv()
        added = sum_buf[t, 0].astype(jnp.float32)
        for g in range(1, RING):
            added = added + sum_buf[t, g].astype(jnp.float32)
        return (added * scale).astype(jnp.bfloat16)

    start = finish(0)
    edge_out[...] = start

    @pl.when(tm > 0)
    def _():
        edge_copy().start()

    out_ref[:, :LANES] = start
    for t in range(1, tiles):
        out_ref[:, t * LANES : (t + 1) * LANES] = finish(t)

    @pl.when(last)
    def _():
        edge_in[...] = jnp.zeros((dms, LANES), jnp.bfloat16)

    @pl.when(jnp.logical_not(last))
    def _():
        edge_copy().wait_recv()

    out_ref[:, length:] = edge_in[...]

    for d in NEAR_FIRST:
        own_copy(d, y).wait_send()
        lag_copy(d, z).wait_send()
        for t in range(tiles):
            part_copy(t, d, z).wait_send()

    @pl.when(tm > 0)
    def _():
        for d in (0,) + NEAR_FIRST:
            halo_copy(d, y).wait_send()
        edge_copy().wait_send()


def boxcar_kernel(widths_ref, series_ref, out_ref, woven):
    length = out_ref.shape[1]
    count = widths_ref.shape[0]
    dms = series_ref.shape[0]
    tiles = length // LANES
    spans = [series_ref[:, h * LANES : (h + 2) * LANES] for h in range(tiles)]
    spans = jnp.concatenate(spans, axis=0)
    lag = iota((2 * LANES, LANES), 0) - iota((2 * LANES, LANES), 1)
    lag = jnp.where(lag < 0, WMAX, lag)
    for i in range(count):
        width = widths_ref[i]
        window = jnp.where(lag < width, 1.0, 0.0).astype(jnp.bfloat16)
        total = jnp.dot(spans, window, preferred_element_type=jnp.float32)
        total = total / jnp.sqrt(jnp.full((1, LANES), width, jnp.int32).astype(jnp.float32))
        for h in range(tiles):
            woven[h, pl.ds(i, dms, stride=count), :] = total[h * dms : (h + 1) * dms]
    for h in range(tiles):
        out_ref[:, h * LANES : (h + 1) * LANES] = woven[h]


def solution(mesh):
    blocks = mesh.shape["tm"]

    def per_device(data, delays, offsets, widths):
        _, chans, length = data.shape
        dms, nsub = offsets.shape
        groups = lax.axis_size("sub")
        per = nsub // groups
        scale = 1.0 / math.sqrt(chans * groups)
        vmem = pl.BlockSpec(memory_space=pltpu.VMEM)
        bf16 = jnp.bfloat16
        dma = pltpu.SemaphoreType.DMA((RING,))
        series = pl.pallas_call(
            functools.partial(dedisperse_kernel, scale, blocks),
            out_shape=jax.ShapeDtypeStruct((dms, length + LANES), bf16),
            in_specs=[pl.BlockSpec(memory_space=pl.ANY)] * 3,
            out_specs=vmem,
            scratch_shapes=[
                pltpu.VMEM((chans, length), bf16),
                pltpu.VMEM((1, chans), jnp.int32),
                pltpu.VMEM((dms, nsub), jnp.int32),
                pltpu.VMEM((RING, dms, LANES), bf16),
                pltpu.VMEM((RING, dms, LANES), bf16),
                pltpu.VMEM((RING, per, length), bf16),
                pltpu.VMEM((per, LANES), bf16),
                pltpu.VMEM((RING, per, LANES), bf16),
                pltpu.VMEM((length + LANES, RING * per), jnp.float32),
                pltpu.VMEM((length // LANES, RING, dms, LANES), bf16),
                pltpu.VMEM((length // LANES, RING, dms, LANES), bf16),
                pltpu.VMEM((dms, LANES), bf16),
                pltpu.VMEM((dms, LANES), bf16),
            ]
            + [dma] * 6
            + [pltpu.SemaphoreType.DMA((RING * (length // LANES),))] * 2
            + [pltpu.SemaphoreType.DMA((1,))] * 2
            + [pltpu.SemaphoreType.DMA((3,))],
            compiler_params=pltpu.CompilerParams(collective_id=0, has_side_effects=True),
        )(data[0], delays[None, :], offsets)
        count = widths.shape[0]
        out = pl.pallas_call(
            boxcar_kernel,
            out_shape=jax.ShapeDtypeStruct((dms * count, length), jnp.float32),
            in_specs=[pl.BlockSpec(memory_space=pltpu.SMEM), vmem],
            out_specs=vmem,
            scratch_shapes=[pltpu.VMEM((length // LANES, dms * count, LANES), jnp.float32)],
        )(widths, series)
        return out.reshape(dms, 1, count, length)

    placed = (P(None, "sub", "tm"), P("sub"), P("sub", None), P())
    return jax.shard_map(
        per_device,
        mesh=mesh,
        in_specs=placed,
        out_specs=P("sub", None, None, "tm"),
        check_vma=False,
    )
```

```python
import functools
import math

import jax
import jax.numpy as jnp
from jax import lax
from jax.experimental import pallas as pl
from jax.experimental.pallas import tpu as pltpu
from jax.sharding import PartitionSpec as P

WMAX = 128
DCH = 16
OMAX = 96
RING = 8
LANES = 128
EDGE = 112
MESH = pl.DeviceIdType.MESH
FAR_FIRST = (4, 3, 5, 2, 6, 1, 7)
NEAR_FIRST = (1, 7, 2, 6, 3, 5, 4)


def iota(shape, dim):
    return lax.broadcasted_iota(jnp.int32, shape, dim)


def dedisperse_kernel(
    scale,
    blocks,
    data_hbm,
    delays_hbm,
    offsets_hbm,
    out_ref,
    data_ref,
    delays_ref,
    offsets_ref,
    lag_out,
    lags,
    own_buf,
    halo_out,
    halo_buf,
    turned,
    part_buf,
    sum_buf,
    edge_out,
    edge_in,
    send_own,
    recv_own,
    send_halo,
    recv_halo,
    send_lag,
    recv_lag,
    send_part,
    recv_part,
    send_edge,
    recv_edge,
    load,
):
    sub = lax.axis_index("sub")
    tm = lax.axis_index("tm")
    z, y = sub // RING, sub % RING
    chans, length = data_ref.shape
    per = own_buf.shape[1]
    dms = lag_out.shape[1]
    first, last = tm == 0, tm == blocks - 1

    def along_y(d):
        return z * RING + lax.rem(y + d, RING)

    def along_z(d):
        return lax.rem(z + d, RING) * RING + y

    barrier = pltpu.get_barrier_semaphore()

    def fetch(i, source, target):
        return pltpu.make_async_copy(source, target, load.at[i])

    fetch(0, data_hbm, data_ref).start()
    fetch(1, delays_hbm, delays_ref).start()
    fetch(2, offsets_hbm, offsets_ref).start()

    for d in FAR_FIRST:
        pl.semaphore_signal(barrier, inc=1, device_id=(along_y(d), tm), device_id_type=MESH)
        pl.semaphore_signal(barrier, inc=1, device_id=(along_z(d), tm), device_id_type=MESH)

    @pl.when(jnp.logical_not(last))
    def _():
        for d in FAR_FIRST + (0,):
            pl.semaphore_signal(barrier, inc=1, device_id=(along_y(d), tm + 1), device_id_type=MESH)

    fetch(2, offsets_hbm, offsets_ref).wait()
    for g in range(RING):
        lag_out[g] = offsets_ref[:, g * LANES : (g + 1) * LANES].astype(jnp.float32).astype(jnp.bfloat16)
    lags[z] = lag_out[z]

    fetch(0, data_hbm, data_ref).wait()
    fetch(1, delays_hbm, delays_ref).wait()
    pick, chan = iota((DCH * per, chans), 0), iota((DCH * per, chans), 1)
    same = jnp.logical_and(chan // (chans // per) == pick % per, delays_ref[...] == pick // per)
    spread = jnp.dot(
        jnp.where(same, 1.0, 0.0).astype(jnp.bfloat16), data_ref[...], preferred_element_type=jnp.float32
    )
    wide = length + LANES
    summed = jnp.zeros((per, wide), jnp.float32)
    for j in range(DCH):
        part = jnp.concatenate([jnp.zeros((per, LANES), jnp.float32), spread[j * per : (j + 1) * per]], axis=1)
        summed = summed + (pltpu.roll(part, wide - j, 1) if j else part)
    own_buf[y] = summed[:, LANES:].astype(jnp.bfloat16)
    halo_out[...] = jnp.where(
        iota((per, LANES), 1) < EDGE, summed[:, LANES : 2 * LANES], summed[:, :LANES]
    ).astype(jnp.bfloat16)

    pl.semaphore_wait(
        barrier,
        2 * (RING - 1) + jnp.where(first, 0, RING),
    )

    def lag_copy(d, source):
        g = lax.rem(z + d, RING)
        return pltpu.make_async_remote_copy(
            src_ref=lag_out.at[g],
            dst_ref=lags.at[source],
            send_sem=send_lag.at[d],
            recv_sem=recv_lag.at[source],
            device_id=(along_z(d), tm),
            device_id_type=MESH,
        )

    def own_copy(d, source):
        return pltpu.make_async_remote_copy(
            src_ref=own_buf.at[y],
            dst_ref=own_buf.at[source],
            send_sem=send_own.at[d],
            recv_sem=recv_own.at[source],
            device_id=(along_y(d), tm),
            device_id_type=MESH,
        )

    def halo_copy(d, source):
        return pltpu.make_async_remote_copy(
            src_ref=halo_out,
            dst_ref=halo_buf.at[source],
            send_sem=send_halo.at[d],
            recv_sem=recv_halo.at[source],
            device_id=(along_y(d), tm - 1),
            device_id_type=MESH,
        )

    for d in FAR_FIRST:
        own_copy(d, y).start()
        lag_copy(d, z).start()

    @pl.when(tm > 0)
    def _():
        for d in FAR_FIRST + (0,):
            halo_copy(d, y).start()

    @pl.when(last)
    def _():
        halo_buf[...] = jnp.zeros(halo_buf.shape, halo_buf.dtype)

    for d in NEAR_FIRST:
        lag_copy(d, lax.rem(z + d, RING)).wait_recv()
        own_copy(d, lax.rem(y + d, RING)).wait_recv()

    rows = RING * per
    turned[:length] = own_buf[...].reshape(rows, length).astype(jnp.float32).T

    table = lags[...].reshape(RING * dms, rows).astype(jnp.float32).T.astype(jnp.bfloat16)

    def part_copy(t, d, source):
        return pltpu.make_async_remote_copy(
            src_ref=part_buf.at[t, lax.rem(z + d, RING)],
            dst_ref=sum_buf.at[t, source],
            send_sem=send_part.at[t * RING + d],
            recv_sem=recv_part.at[t * RING + source],
            device_id=(along_z(d), tm),
            device_id_type=MESH,
        )

    def edge_copy():
        return pltpu.make_async_remote_copy(
            src_ref=edge_out,
            dst_ref=edge_in,
            send_sem=send_edge.at[0],
            recv_sem=recv_edge.at[0],
            device_id=(sub, tm - 1),
            device_id_type=MESH,
        )

    def add_halo():
        @pl.when(jnp.logical_not(last))
        def _():
            for d in (0,) + NEAR_FIRST:
                halo_copy(d, lax.rem(y + d, RING)).wait_recv()

        halo = halo_buf[...].reshape(rows, LANES).astype(jnp.float32)
        edge = jnp.where(iota((rows, LANES), 1) >= EDGE, halo, 0.0)
        tail = own_buf[:, :, length - LANES :].reshape(rows, LANES).astype(jnp.float32) + edge
        turned[length - LANES : length] = tail.astype(jnp.bfloat16).astype(jnp.float32).T
        turned[length:] = halo.T

    tiles = length // LANES

    def tile(t, carry):
        pl.when(t == tiles - 1)(add_halo)
        masks, windows = [], []
        for j in range(OMAX + 1):
            masks.append(jnp.where(table == jnp.bfloat16(j), jnp.bfloat16(1), jnp.bfloat16(0)))
            windows.append(turned[pl.ds(t * LANES + j, LANES), :].astype(jnp.bfloat16))
        total = jnp.dot(
            jnp.concatenate(windows, axis=1),
            jnp.concatenate(masks, axis=0),
            preferred_element_type=jnp.float32,
        )
        part_buf[t] = total.T.astype(jnp.bfloat16).reshape(RING, dms, LANES)
        for d in FAR_FIRST:
            part_copy(t, d, z).start()

        sum_buf[t, z] = part_buf[t, z]
        return carry

    lax.fori_loop(0, tiles, tile, 0)

    def finish(t):
        for d in NEAR_FIRST:
            part_copy(t, d, lax.rem(z + d, RING)).wait_recv()
        added = sum_buf[t, 0].astype(jnp.float32)
        for g in range(1, RING):
            added = added + sum_buf[t, g].astype(jnp.float32)
        return (added * scale).astype(jnp.bfloat16)

    start = finish(0)
    edge_out[...] = start

    @pl.when(tm > 0)
    def _():
        edge_copy().start()

    out_ref[:, :LANES] = start
    for t in range(1, tiles):
        out_ref[:, t * LANES : (t + 1) * LANES] = finish(t)

    @pl.when(last)
    def _():
        edge_in[...] = jnp.zeros((dms, LANES), jnp.bfloat16)

    @pl.when(jnp.logical_not(last))
    def _():
        edge_copy().wait_recv()

    out_ref[:, length:] = edge_in[...]

    for d in NEAR_FIRST:
        own_copy(d, y).wait_send()
        lag_copy(d, z).wait_send()
        for t in range(tiles):
            part_copy(t, d, z).wait_send()

    @pl.when(tm > 0)
    def _():
        for d in (0,) + NEAR_FIRST:
            halo_copy(d, y).wait_send()
        edge_copy().wait_send()


def boxcar_kernel(widths_ref, series_ref, out_ref, woven):
    length = out_ref.shape[1]
    count = widths_ref.shape[0]
    dms = series_ref.shape[0]
    tiles = length // LANES
    spans = [series_ref[:, h * LANES : (h + 2) * LANES] for h in range(tiles)]
    spans = jnp.concatenate(spans, axis=0)
    lag = iota((2 * LANES, LANES), 0) - iota((2 * LANES, LANES), 1)
    lag = jnp.where(lag < 0, WMAX, lag)
    for i in range(count):
        width = widths_ref[i]
        window = jnp.where(lag < width, 1.0, 0.0).astype(jnp.bfloat16)
        total = jnp.dot(spans, window, preferred_element_type=jnp.float32)
        total = total / jnp.sqrt(jnp.full((1, LANES), width, jnp.int32).astype(jnp.float32))
        for h in range(tiles):
            woven[h, pl.ds(i, dms, stride=count), :] = total[h * dms : (h + 1) * dms]
    for h in range(tiles):
        out_ref[:, h * LANES : (h + 1) * LANES] = woven[h]


def solution(mesh):
    blocks = mesh.shape["tm"]

    def per_device(data, delays, offsets, widths):
        _, chans, length = data.shape
        dms, nsub = offsets.shape
        groups = lax.axis_size("sub")
        per = nsub // groups
        scale = 1.0 / math.sqrt(chans * groups)
        vmem = pl.BlockSpec(memory_space=pltpu.VMEM)
        bf16 = jnp.bfloat16
        dma = pltpu.SemaphoreType.DMA((RING,))
        series = pl.pallas_call(
            functools.partial(dedisperse_kernel, scale, blocks),
            out_shape=jax.ShapeDtypeStruct((dms, length + LANES), bf16),
            in_specs=[pl.BlockSpec(memory_space=pl.ANY)] * 3,
            out_specs=vmem,
            scratch_shapes=[
                pltpu.VMEM((chans, length), bf16),
                pltpu.VMEM((1, chans), jnp.int32),
                pltpu.VMEM((dms, nsub), jnp.int32),
                pltpu.VMEM((RING, dms, LANES), bf16),
                pltpu.VMEM((RING, dms, LANES), bf16),
                pltpu.VMEM((RING, per, length), bf16),
                pltpu.VMEM((per, LANES), bf16),
                pltpu.VMEM((RING, per, LANES), bf16),
                pltpu.VMEM((length + LANES, RING * per), jnp.float32),
                pltpu.VMEM((length // LANES, RING, dms, LANES), bf16),
                pltpu.VMEM((length // LANES, RING, dms, LANES), bf16),
                pltpu.VMEM((dms, LANES), bf16),
                pltpu.VMEM((dms, LANES), bf16),
            ]
            + [dma] * 6
            + [pltpu.SemaphoreType.DMA((RING * (length // LANES),))] * 2
            + [pltpu.SemaphoreType.DMA((1,))] * 2
            + [pltpu.SemaphoreType.DMA((3,))],
            compiler_params=pltpu.CompilerParams(collective_id=0, has_side_effects=True),
        )(data[0], delays[None, :], offsets)
        count = widths.shape[0]
        out = pl.pallas_call(
            boxcar_kernel,
            out_shape=jax.ShapeDtypeStruct((dms * count, length), jnp.float32),
            in_specs=[pl.BlockSpec(memory_space=pltpu.SMEM), vmem],
            out_specs=vmem,
            scratch_shapes=[pltpu.VMEM((length // LANES, dms * count, LANES), jnp.float32)],
        )(widths, series)
        return out.reshape(dms, 1, count, length)

    placed = (P(None, "sub", "tm"), P("sub"), P("sub", None), P())
    return jax.shard_map(
        per_device,
        mesh=mesh,
        in_specs=placed,
        out_specs=P("sub", None, None, "tm"),
        check_vma=False,
    )
```

```python
import functools
import math

import jax
import jax.numpy as jnp
from jax import lax
from jax.experimental import pallas as pl
from jax.experimental.pallas import tpu as pltpu
from jax.sharding import PartitionSpec as P

WMAX = 128
DCH = 16
OMAX = 96
RING = 8
LANES = 128
EDGE = 112
MESH = pl.DeviceIdType.MESH
FAR_FIRST = (4, 3, 5, 2, 6, 1, 7)
NEAR_FIRST = (1, 7, 2, 6, 3, 5, 4)


def iota(shape, dim):
    return lax.broadcasted_iota(jnp.int32, shape, dim)


def dedisperse_kernel(
    scale,
    blocks,
    data_hbm,
    delays_hbm,
    offsets_hbm,
    out_ref,
    data_ref,
    delays_ref,
    offsets_ref,
    lag_out,
    lags,
    own_buf,
    halo_out,
    halo_buf,
    turned,
    part_buf,
    sum_buf,
    edge_out,
    edge_in,
    send_own,
    recv_own,
    send_halo,
    recv_halo,
    send_lag,
    recv_lag,
    send_part,
    recv_part,
    send_edge,
    recv_edge,
    load,
):
    sub = lax.axis_index("sub")
    tm = lax.axis_index("tm")
    z, y = sub // RING, sub % RING
    chans, length = data_ref.shape
    per = own_buf.shape[1]
    dms = lag_out.shape[1]
    first, last = tm == 0, tm == blocks - 1

    def along_y(d):
        return z * RING + lax.rem(y + d, RING)

    def along_z(d):
        return lax.rem(z + d, RING) * RING + y

    barrier = pltpu.get_barrier_semaphore()

    def fetch(i, source, target):
        return pltpu.make_async_copy(source, target, load.at[i])

    fetch(0, data_hbm, data_ref).start()
    fetch(1, delays_hbm, delays_ref).start()
    fetch(2, offsets_hbm, offsets_ref).start()

    for d in FAR_FIRST:
        pl.semaphore_signal(barrier, inc=1, device_id=(along_y(d), tm), device_id_type=MESH)
        pl.semaphore_signal(barrier, inc=1, device_id=(along_z(d), tm), device_id_type=MESH)

    @pl.when(jnp.logical_not(last))
    def _():
        pl.semaphore_signal(barrier, inc=1, device_id=(sub, tm + 1), device_id_type=MESH)

    fetch(2, offsets_hbm, offsets_ref).wait()
    for g in range(RING):
        lag_out[g] = offsets_ref[:, g * LANES : (g + 1) * LANES].astype(jnp.float32).astype(jnp.bfloat16)
    lags[z] = lag_out[z]

    fetch(0, data_hbm, data_ref).wait()
    fetch(1, delays_hbm, delays_ref).wait()
    pick, chan = iota((DCH * per, chans), 0), iota((DCH * per, chans), 1)
    same = jnp.logical_and(chan // (chans // per) == pick % per, delays_ref[...] == pick // per)
    spread = jnp.dot(
        jnp.where(same, 1.0, 0.0).astype(jnp.bfloat16), data_ref[...], preferred_element_type=jnp.float32
    )
    wide = length + LANES
    summed = jnp.zeros((per, wide), jnp.float32)
    for j in range(DCH):
        part = jnp.concatenate([jnp.zeros((per, LANES), jnp.float32), spread[j * per : (j + 1) * per]], axis=1)
        summed = summed + (pltpu.roll(part, wide - j, 1) if j else part)
    own_buf[y] = summed[:, LANES:].astype(jnp.bfloat16)
    halo_out[...] = jnp.where(
        iota((per, LANES), 1) < EDGE, summed[:, LANES : 2 * LANES], summed[:, :LANES]
    ).astype(jnp.bfloat16)

    pl.semaphore_wait(barrier, 2 * (RING - 1) + jnp.where(first, 0, 1))

    def lag_copy(d, source):
        g = lax.rem(z + d, RING)
        return pltpu.make_async_remote_copy(
            src_ref=lag_out.at[g],
            dst_ref=lags.at[source],
            send_sem=send_lag.at[d],
            recv_sem=recv_lag.at[source],
            device_id=(along_z(d), tm),
            device_id_type=MESH,
        )

    def own_copy(d, source):
        return pltpu.make_async_remote_copy(
            src_ref=own_buf.at[y],
            dst_ref=own_buf.at[source],
            send_sem=send_own.at[d],
            recv_sem=recv_own.at[source],
            device_id=(along_y(d), tm),
            device_id_type=MESH,
        )

    def hop_copy():
        return pltpu.make_async_remote_copy(
            src_ref=halo_out,
            dst_ref=halo_buf.at[y],
            send_sem=send_edge.at[1],
            recv_sem=recv_edge.at[1],
            device_id=(sub, tm - 1),
            device_id_type=MESH,
        )

    def halo_copy(d, source):
        return pltpu.make_async_remote_copy(
            src_ref=halo_buf.at[y],
            dst_ref=halo_buf.at[source],
            send_sem=send_halo.at[d],
            recv_sem=recv_halo.at[source],
            device_id=(along_y(d), tm),
            device_id_type=MESH,
        )

    @pl.when(tm > 0)
    def _():
        hop_copy().start()

    for d in FAR_FIRST:
        own_copy(d, y).start()
        lag_copy(d, z).start()

    @pl.when(last)
    def _():
        halo_buf[...] = jnp.zeros(halo_buf.shape, halo_buf.dtype)

    @pl.when(jnp.logical_not(last))
    def _():
        hop_copy().wait_recv()
        for d in FAR_FIRST:
            halo_copy(d, y).start()

    rows = RING * per
    for d in NEAR_FIRST:
        lag_copy(d, lax.rem(z + d, RING)).wait_recv()
    table = lags[...].reshape(RING * dms, rows).astype(jnp.float32).T.astype(jnp.bfloat16)

    for d in NEAR_FIRST:
        own_copy(d, lax.rem(y + d, RING)).wait_recv()
    turned[:length] = own_buf[...].reshape(rows, length).astype(jnp.float32).T

    def part_copy(t, d, source):
        return pltpu.make_async_remote_copy(
            src_ref=part_buf.at[t, lax.rem(z + d, RING)],
            dst_ref=sum_buf.at[t, source],
            send_sem=send_part.at[t * RING + d],
            recv_sem=recv_part.at[t * RING + source],
            device_id=(along_z(d), tm),
            device_id_type=MESH,
        )

    def edge_copy():
        return pltpu.make_async_remote_copy(
            src_ref=edge_out,
            dst_ref=edge_in,
            send_sem=send_edge.at[0],
            recv_sem=recv_edge.at[0],
            device_id=(sub, tm - 1),
            device_id_type=MESH,
        )

    def add_halo():
        @pl.when(jnp.logical_not(last))
        def _():
            for d in NEAR_FIRST:
                halo_copy(d, lax.rem(y + d, RING)).wait_recv()

        halo = halo_buf[...].reshape(rows, LANES).astype(jnp.float32)
        edge = jnp.where(iota((rows, LANES), 1) >= EDGE, halo, 0.0)
        tail = own_buf[:, :, length - LANES :].reshape(rows, LANES).astype(jnp.float32) + edge
        turned[length - LANES : length] = tail.astype(jnp.bfloat16).astype(jnp.float32).T
        turned[length:] = halo.T

    tiles = length // LANES

    def tile(t, carry):
        pl.when(t == tiles - 1)(add_halo)
        masks, windows = [], []
        for j in range(OMAX + 1):
            masks.append(jnp.where(table == jnp.bfloat16(j), jnp.bfloat16(1), jnp.bfloat16(0)))
            windows.append(turned[pl.ds(t * LANES + j, LANES), :].astype(jnp.bfloat16))
        total = jnp.dot(
            jnp.concatenate(windows, axis=1),
            jnp.concatenate(masks, axis=0),
            preferred_element_type=jnp.float32,
        )
        part_buf[t] = total.T.astype(jnp.bfloat16).reshape(RING, dms, LANES)
        for d in FAR_FIRST:
            part_copy(t, d, z).start()

        sum_buf[t, z] = part_buf[t, z]
        return carry

    lax.fori_loop(0, tiles, tile, 0)

    def finish(t):
        for d in NEAR_FIRST:
            part_copy(t, d, lax.rem(z + d, RING)).wait_recv()
        added = sum_buf[t, 0].astype(jnp.float32)
        for g in range(1, RING):
            added = added + sum_buf[t, g].astype(jnp.float32)
        return (added * scale).astype(jnp.bfloat16)

    start = finish(0)
    edge_out[...] = start

    @pl.when(tm > 0)
    def _():
        edge_copy().start()

    out_ref[:, :LANES] = start
    for t in range(1, tiles):
        out_ref[:, t * LANES : (t + 1) * LANES] = finish(t)

    @pl.when(last)
    def _():
        edge_in[...] = jnp.zeros((dms, LANES), jnp.bfloat16)

    @pl.when(jnp.logical_not(last))
    def _():
        edge_copy().wait_recv()

    out_ref[:, length:] = edge_in[...]

    for d in NEAR_FIRST:
        own_copy(d, y).wait_send()
        lag_copy(d, z).wait_send()
        for t in range(tiles):
            part_copy(t, d, z).wait_send()

    @pl.when(jnp.logical_not(last))
    def _():
        for d in NEAR_FIRST:
            halo_copy(d, y).wait_send()

    @pl.when(tm > 0)
    def _():
        hop_copy().wait_send()
        edge_copy().wait_send()


def boxcar_kernel(widths_ref, series_ref, out_ref, woven):
    length = out_ref.shape[1]
    count = widths_ref.shape[0]
    dms = series_ref.shape[0]
    tiles = length // LANES
    spans = [series_ref[:, h * LANES : (h + 2) * LANES] for h in range(tiles)]
    spans = jnp.concatenate(spans, axis=0)
    lag = iota((2 * LANES, LANES), 0) - iota((2 * LANES, LANES), 1)
    lag = jnp.where(lag < 0, WMAX, lag)
    for i in range(count):
        width = widths_ref[i]
        window = jnp.where(lag < width, 1.0, 0.0).astype(jnp.bfloat16)
        total = jnp.dot(spans, window, preferred_element_type=jnp.float32)
        total = total / jnp.sqrt(jnp.full((1, LANES), width, jnp.int32).astype(jnp.float32))
        for h in range(tiles):
            woven[h, pl.ds(i, dms, stride=count), :] = total[h * dms : (h + 1) * dms]
    for h in range(tiles):
        out_ref[:, h * LANES : (h + 1) * LANES] = woven[h]


def solution(mesh):
    blocks = mesh.shape["tm"]

    def per_device(data, delays, offsets, widths):
        _, chans, length = data.shape
        dms, nsub = offsets.shape
        groups = lax.axis_size("sub")
        per = nsub // groups
        scale = 1.0 / math.sqrt(chans * groups)
        vmem = pl.BlockSpec(memory_space=pltpu.VMEM)
        bf16 = jnp.bfloat16
        dma = pltpu.SemaphoreType.DMA((RING,))
        series = pl.pallas_call(
            functools.partial(dedisperse_kernel, scale, blocks),
            out_shape=jax.ShapeDtypeStruct((dms, length + LANES), bf16),
            in_specs=[pl.BlockSpec(memory_space=pl.ANY)] * 3,
            out_specs=vmem,
            scratch_shapes=[
                pltpu.VMEM((chans, length), bf16),
                pltpu.VMEM((1, chans), jnp.int32),
                pltpu.VMEM((dms, nsub), jnp.int32),
                pltpu.VMEM((RING, dms, LANES), bf16),
                pltpu.VMEM((RING, dms, LANES), bf16),
                pltpu.VMEM((RING, per, length), bf16),
                pltpu.VMEM((per, LANES), bf16),
                pltpu.VMEM((RING, per, LANES), bf16),
                pltpu.VMEM((length + LANES, RING * per), jnp.float32),
                pltpu.VMEM((length // LANES, RING, dms, LANES), bf16),
                pltpu.VMEM((length // LANES, RING, dms, LANES), bf16),
                pltpu.VMEM((dms, LANES), bf16),
                pltpu.VMEM((dms, LANES), bf16),
            ]
            + [dma] * 6
            + [pltpu.SemaphoreType.DMA((RING * (length // LANES),))] * 2
            + [pltpu.SemaphoreType.DMA((2,))] * 2
            + [pltpu.SemaphoreType.DMA((3,))],
            compiler_params=pltpu.CompilerParams(collective_id=0, has_side_effects=True),
        )(data[0], delays[None, :], offsets)
        count = widths.shape[0]
        out = pl.pallas_call(
            boxcar_kernel,
            out_shape=jax.ShapeDtypeStruct((dms * count, length), jnp.float32),
            in_specs=[pl.BlockSpec(memory_space=pltpu.SMEM), vmem],
            out_specs=vmem,
            scratch_shapes=[pltpu.VMEM((length // LANES, dms * count, LANES), jnp.float32)],
        )(widths, series)
        return out.reshape(dms, 1, count, length)

    placed = (P(None, "sub", "tm"), P("sub"), P("sub", None), P())
    return jax.shard_map(
        per_device,
        mesh=mesh,
        in_specs=placed,
        out_specs=P("sub", None, None, "tm"),
        check_vma=False,
    )
```

```python
import functools
import math

import jax
import jax.numpy as jnp
from jax import lax
from jax.experimental import pallas as pl
from jax.experimental.pallas import tpu as pltpu
from jax.sharding import PartitionSpec as P

WMAX = 128
DCH = 16
OMAX = 96
RING = 8
LANES = 128
EDGE = 112
MESH = pl.DeviceIdType.MESH
FAR_FIRST = (4, 3, 5, 2, 6, 1, 7)
NEAR_FIRST = (1, 7, 2, 6, 3, 5, 4)
NEAR = (2, 6, 1, 7)
RELAYS = {3: (1, 2, 7), 5: (7, 6, 1), 4: (2, 2, 6)}
LATE = (2, 3, 5, 4)


def iota(shape, dim):
    return lax.broadcasted_iota(jnp.int32, shape, dim)


def dedisperse_kernel(
    scale,
    blocks,
    data_hbm,
    delays_hbm,
    offsets_hbm,
    out_ref,
    data_ref,
    delays_ref,
    offsets_ref,
    lag_out,
    lags,
    passing,
    own_buf,
    halo_out,
    halo_buf,
    turned,
    part_buf,
    sum_buf,
    edge_out,
    edge_in,
    send_own,
    recv_own,
    send_halo,
    recv_halo,
    send_lag,
    recv_lag,
    send_pass,
    recv_pass,
    send_part,
    recv_part,
    send_edge,
    recv_edge,
    load,
):
    sub = lax.axis_index("sub")
    tm = lax.axis_index("tm")
    z, y = sub // RING, sub % RING
    chans, length = data_ref.shape
    per = own_buf.shape[1]
    dms = lag_out.shape[1]
    first, last = tm == 0, tm == blocks - 1

    def along_y(d):
        return z * RING + lax.rem(y + d, RING)

    def along_z(d):
        return lax.rem(z + d, RING) * RING + y

    barrier = pltpu.get_barrier_semaphore()

    def fetch(i, source, target):
        return pltpu.make_async_copy(source, target, load.at[i])

    fetch(0, data_hbm, data_ref).start()
    fetch(1, delays_hbm, delays_ref).start()
    fetch(2, offsets_hbm, offsets_ref).start()

    for d in NEAR:
        pl.semaphore_signal(barrier, inc=1, device_id=(along_y(d), tm), device_id_type=MESH)
        pl.semaphore_signal(barrier, inc=1, device_id=(along_z(d), tm), device_id_type=MESH)

    @pl.when(jnp.logical_not(last))
    def _():
        pl.semaphore_signal(barrier, inc=1, device_id=(sub, tm + 1), device_id_type=MESH)

    fetch(2, offsets_hbm, offsets_ref).wait()
    for g in range(RING):
        lag_out[g] = offsets_ref[:, g * LANES : (g + 1) * LANES].astype(jnp.float32).astype(jnp.bfloat16)
    lags[z] = lag_out[z]

    fetch(0, data_hbm, data_ref).wait()
    fetch(1, delays_hbm, delays_ref).wait()
    pick, chan = iota((DCH * per, chans), 0), iota((DCH * per, chans), 1)
    same = jnp.logical_and(chan // (chans // per) == pick % per, delays_ref[...] == pick // per)
    spread = jnp.dot(
        jnp.where(same, 1.0, 0.0).astype(jnp.bfloat16), data_ref[...], preferred_element_type=jnp.float32
    )
    wide = length + LANES
    summed = jnp.zeros((per, wide), jnp.float32)
    for j in range(DCH):
        part = jnp.concatenate([jnp.zeros((per, LANES), jnp.float32), spread[j * per : (j + 1) * per]], axis=1)
        summed = summed + (pltpu.roll(part, wide - j, 1) if j else part)
    own_buf[y] = summed[:, LANES:].astype(jnp.bfloat16)
    halo_out[...] = jnp.where(
        iota((per, LANES), 1) < EDGE, summed[:, LANES : 2 * LANES], summed[:, :LANES]
    ).astype(jnp.bfloat16)

    pl.semaphore_wait(barrier, 2 * len(NEAR) + jnp.where(first, 0, 1))

    def lag_copy(d, source):
        g = lax.rem(z + d, RING)
        return pltpu.make_async_remote_copy(
            src_ref=lag_out.at[g],
            dst_ref=lags.at[source],
            send_sem=send_lag.at[d],
            recv_sem=recv_lag.at[source],
            device_id=(along_z(d), tm),
            device_id_type=MESH,
        )

    def pass_copy(far):
        step, _, _ = RELAYS[far]
        return pltpu.make_async_remote_copy(
            src_ref=lag_out.at[lax.rem(z + far, RING)],
            dst_ref=passing.at[far - 3],
            send_sem=send_lag.at[far],
            recv_sem=recv_pass.at[far],
            device_id=(along_z(step), tm),
            device_id_type=MESH,
        )

    def onward_copy(far):
        _, step, source = RELAYS[far]
        source = lax.rem(z + source, RING)
        return pltpu.make_async_remote_copy(
            src_ref=passing.at[far - 3],
            dst_ref=lags.at[source],
            send_sem=send_pass.at[far],
            recv_sem=recv_lag.at[source],
            device_id=(along_z(step), tm),
            device_id_type=MESH,
        )

    def own_copy(slot, step, source):
        source = lax.rem(y + source, RING)
        return pltpu.make_async_remote_copy(
            src_ref=own_buf.at[source],
            dst_ref=own_buf.at[source],
            send_sem=send_own.at[slot],
            recv_sem=recv_own.at[source],
            device_id=(along_y(step), tm),
            device_id_type=MESH,
        )

    def hop_copy():
        return pltpu.make_async_remote_copy(
            src_ref=halo_out,
            dst_ref=halo_buf.at[y],
            send_sem=send_edge.at[1],
            recv_sem=recv_edge.at[1],
            device_id=(sub, tm - 1),
            device_id_type=MESH,
        )

    def halo_copy(slot, step, source):
        source = lax.rem(y + source, RING)
        return pltpu.make_async_remote_copy(
            src_ref=halo_buf.at[source],
            dst_ref=halo_buf.at[source],
            send_sem=send_halo.at[slot],
            recv_sem=recv_halo.at[source],
            device_id=(along_y(step), tm),
            device_id_type=MESH,
        )

    @pl.when(tm > 0)
    def _():
        hop_copy().start()

    for far in RELAYS:
        pass_copy(far).start()
    for d in NEAR:
        own_copy(d, d, 0).start()
        lag_copy(d, z).start()

    @pl.when(last)
    def _():
        halo_buf[...] = jnp.zeros(halo_buf.shape, halo_buf.dtype)

    @pl.when(jnp.logical_not(last))
    def _():
        hop_copy().wait_recv()
        for d in NEAR:
            halo_copy(d, d, 0).start()

    for far, (_, step, source) in RELAYS.items():
        own_copy(far, step, source).wait_recv()
        own_copy(far, step, source).start()
        pass_copy(far).wait_recv()
        onward_copy(far).start()

    @pl.when(jnp.logical_not(last))
    def _():
        for far, (_, step, source) in RELAYS.items():
            halo_copy(far, step, source).wait_recv()
            halo_copy(far, step, source).start()

    rows = RING * per
    for d in NEAR_FIRST:
        lag_copy(d, lax.rem(z + d, RING)).wait_recv()
    table = lags[...].reshape(RING * dms, rows).astype(jnp.float32).T.astype(jnp.bfloat16)

    for d in LATE:
        own_copy(d, 1, d).wait_recv()
    turned[:length] = own_buf[...].reshape(rows, length).astype(jnp.float32).T

    def part_copy(t, d, source):
        return pltpu.make_async_remote_copy(
            src_ref=part_buf.at[t, lax.rem(z + d, RING)],
            dst_ref=sum_buf.at[t, source],
            send_sem=send_part.at[t * RING + d],
            recv_sem=recv_part.at[t * RING + source],
            device_id=(along_z(d), tm),
            device_id_type=MESH,
        )

    def edge_copy():
        return pltpu.make_async_remote_copy(
            src_ref=edge_out,
            dst_ref=edge_in,
            send_sem=send_edge.at[0],
            recv_sem=recv_edge.at[0],
            device_id=(sub, tm - 1),
            device_id_type=MESH,
        )

    def add_halo():
        @pl.when(jnp.logical_not(last))
        def _():
            for d in LATE:
                halo_copy(d, 1, d).wait_recv()

        halo = halo_buf[...].reshape(rows, LANES).astype(jnp.float32)
        edge = jnp.where(iota((rows, LANES), 1) >= EDGE, halo, 0.0)
        tail = own_buf[:, :, length - LANES :].reshape(rows, LANES).astype(jnp.float32) + edge
        turned[length - LANES : length] = tail.astype(jnp.bfloat16).astype(jnp.float32).T
        turned[length:] = halo.T

    tiles = length // LANES

    def tile(t, carry):
        pl.when(t == tiles - 1)(add_halo)
        masks, windows = [], []
        for j in range(OMAX + 1):
            masks.append(jnp.where(table == jnp.bfloat16(j), jnp.bfloat16(1), jnp.bfloat16(0)))
            windows.append(turned[pl.ds(t * LANES + j, LANES), :].astype(jnp.bfloat16))
        total = jnp.dot(
            jnp.concatenate(windows, axis=1),
            jnp.concatenate(masks, axis=0),
            preferred_element_type=jnp.float32,
        )
        part_buf[t] = total.T.astype(jnp.bfloat16).reshape(RING, dms, LANES)
        for d in FAR_FIRST:
            part_copy(t, d, z).start()

        sum_buf[t, z] = part_buf[t, z]
        return carry

    lax.fori_loop(0, tiles, tile, 0)

    def finish(t):
        for d in NEAR_FIRST:
            part_copy(t, d, lax.rem(z + d, RING)).wait_recv()
        added = sum_buf[t, 0].astype(jnp.float32)
        for g in range(1, RING):
            added = added + sum_buf[t, g].astype(jnp.float32)
        return (added * scale).astype(jnp.bfloat16)

    start = finish(0)
    edge_out[...] = start

    @pl.when(tm > 0)
    def _():
        edge_copy().start()

    out_ref[:, :LANES] = start
    for t in range(1, tiles):
        out_ref[:, t * LANES : (t + 1) * LANES] = finish(t)

    @pl.when(last)
    def _():
        edge_in[...] = jnp.zeros((dms, LANES), jnp.bfloat16)

    @pl.when(jnp.logical_not(last))
    def _():
        edge_copy().wait_recv()

    out_ref[:, length:] = edge_in[...]

    for far in RELAYS:
        onward_copy(far).wait_send()
    for d in NEAR_FIRST:
        own_copy(d, 1, 0).wait_send()
        lag_copy(d, z).wait_send()
        for t in range(tiles):
            part_copy(t, d, z).wait_send()

    @pl.when(jnp.logical_not(last))
    def _():
        for d in NEAR_FIRST:
            halo_copy(d, 1, 0).wait_send()

    @pl.when(tm > 0)
    def _():
        hop_copy().wait_send()
        edge_copy().wait_send()


def boxcar_kernel(widths_ref, series_ref, out_ref, woven):
    length = out_ref.shape[1]
    count = widths_ref.shape[0]
    dms = series_ref.shape[0]
    tiles = length // LANES
    spans = [series_ref[:, h * LANES : (h + 2) * LANES] for h in range(tiles)]
    spans = jnp.concatenate(spans, axis=0)
    lag = iota((2 * LANES, LANES), 0) - iota((2 * LANES, LANES), 1)
    lag = jnp.where(lag < 0, WMAX, lag)
    for i in range(count):
        width = widths_ref[i]
        window = jnp.where(lag < width, 1.0, 0.0).astype(jnp.bfloat16)
        total = jnp.dot(spans, window, preferred_element_type=jnp.float32)
        total = total / jnp.sqrt(jnp.full((1, LANES), width, jnp.int32).astype(jnp.float32))
        for h in range(tiles):
            woven[h, pl.ds(i, dms, stride=count), :] = total[h * dms : (h + 1) * dms]
    for h in range(tiles):
        out_ref[:, h * LANES : (h + 1) * LANES] = woven[h]


def solution(mesh):
    blocks = mesh.shape["tm"]

    def per_device(data, delays, offsets, widths):
        _, chans, length = data.shape
        dms, nsub = offsets.shape
        groups = lax.axis_size("sub")
        per = nsub // groups
        scale = 1.0 / math.sqrt(chans * groups)
        vmem = pl.BlockSpec(memory_space=pltpu.VMEM)
        bf16 = jnp.bfloat16
        dma = pltpu.SemaphoreType.DMA((RING,))
        series = pl.pallas_call(
            functools.partial(dedisperse_kernel, scale, blocks),
            out_shape=jax.ShapeDtypeStruct((dms, length + LANES), bf16),
            in_specs=[pl.BlockSpec(memory_space=pl.ANY)] * 3,
            out_specs=vmem,
            scratch_shapes=[
                pltpu.VMEM((chans, length), bf16),
                pltpu.VMEM((1, chans), jnp.int32),
                pltpu.VMEM((dms, nsub), jnp.int32),
                pltpu.VMEM((RING, dms, LANES), bf16),
                pltpu.VMEM((RING, dms, LANES), bf16),
                pltpu.VMEM((len(RELAYS), dms, LANES), bf16),
                pltpu.VMEM((RING, per, length), bf16),
                pltpu.VMEM((per, LANES), bf16),
                pltpu.VMEM((RING, per, LANES), bf16),
                pltpu.VMEM((length + LANES, RING * per), jnp.float32),
                pltpu.VMEM((length // LANES, RING, dms, LANES), bf16),
                pltpu.VMEM((length // LANES, RING, dms, LANES), bf16),
                pltpu.VMEM((dms, LANES), bf16),
                pltpu.VMEM((dms, LANES), bf16),
            ]
            + [dma] * 8
            + [pltpu.SemaphoreType.DMA((RING * (length // LANES),))] * 2
            + [pltpu.SemaphoreType.DMA((2,))] * 2
            + [pltpu.SemaphoreType.DMA((3,))],
            compiler_params=pltpu.CompilerParams(collective_id=0, has_side_effects=True),
        )(data[0], delays[None, :], offsets)
        count = widths.shape[0]
        out = pl.pallas_call(
            boxcar_kernel,
            out_shape=jax.ShapeDtypeStruct((dms * count, length), jnp.float32),
            in_specs=[pl.BlockSpec(memory_space=pltpu.SMEM), vmem],
            out_specs=vmem,
            scratch_shapes=[pltpu.VMEM((length // LANES, dms * count, LANES), jnp.float32)],
        )(widths, series)
        return out.reshape(dms, 1, count, length)

    placed = (P(None, "sub", "tm"), P("sub"), P("sub", None), P())
    return jax.shard_map(
        per_device,
        mesh=mesh,
        in_specs=placed,
        out_specs=P("sub", None, None, "tm"),
        check_vma=False,
    )
```

```python
import functools
import math

import jax
import jax.numpy as jnp
from jax import lax
from jax.experimental import pallas as pl
from jax.experimental.pallas import tpu as pltpu
from jax.sharding import PartitionSpec as P

WMAX = 128
DCH = 16
OMAX = 96
RING = 8
LANES = 128
EDGE = 112
MESH = pl.DeviceIdType.MESH
FAR_FIRST = (4, 3, 5, 2, 6, 1, 7)
NEAR_FIRST = (1, 7, 2, 6, 3, 5, 4)


def iota(shape, dim):
    return lax.broadcasted_iota(jnp.int32, shape, dim)


def dedisperse_kernel(
    scale,
    blocks,
    data_hbm,
    delays_hbm,
    offsets_hbm,
    out_ref,
    data_ref,
    delays_ref,
    offsets_ref,
    lag_out,
    lags,
    own_buf,
    halo_out,
    halo_in,
    turned,
    part_buf,
    sum_buf,
    edge_out,
    edge_in,
    send_own,
    recv_own,
    send_lag,
    recv_lag,
    send_part,
    recv_part,
    send_edge,
    recv_edge,
    load,
):
    sub = lax.axis_index("sub")
    tm = lax.axis_index("tm")
    z, y = sub // RING, sub % RING
    chans, length = data_ref.shape
    per = own_buf.shape[1]
    dms = lag_out.shape[1]
    first, last = tm == 0, tm == blocks - 1

    def along_y(d):
        return z * RING + lax.rem(y + d, RING)

    def along_z(d):
        return lax.rem(z + d, RING) * RING + y

    barrier = pltpu.get_barrier_semaphore()

    def fetch(i, source, target):
        return pltpu.make_async_copy(source, target, load.at[i])

    fetch(0, data_hbm, data_ref).start()
    fetch(1, delays_hbm, delays_ref).start()
    fetch(2, offsets_hbm, offsets_ref).start()

    for d in FAR_FIRST:
        pl.semaphore_signal(barrier, inc=1, device_id=(along_y(d), tm), device_id_type=MESH)
        pl.semaphore_signal(barrier, inc=1, device_id=(along_z(d), tm), device_id_type=MESH)

    @pl.when(jnp.logical_not(last))
    def _():
        pl.semaphore_signal(barrier, inc=1, device_id=(sub, tm + 1), device_id_type=MESH)

    fetch(2, offsets_hbm, offsets_ref).wait()
    for g in range(RING):
        lag_out[g] = offsets_ref[:, g * LANES : (g + 1) * LANES].astype(jnp.float32).astype(jnp.bfloat16)
    lags[z] = lag_out[z]

    fetch(0, data_hbm, data_ref).wait()
    fetch(1, delays_hbm, delays_ref).wait()
    pick, chan = iota((DCH * per, chans), 0), iota((DCH * per, chans), 1)
    same = jnp.logical_and(chan // (chans // per) == pick % per, delays_ref[...] == pick // per)
    spread = jnp.dot(
        jnp.where(same, 1.0, 0.0).astype(jnp.bfloat16), data_ref[...], preferred_element_type=jnp.float32
    )
    wide = length + LANES
    summed = jnp.zeros((per, wide), jnp.float32)
    for j in range(DCH):
        part = jnp.concatenate([jnp.zeros((per, LANES), jnp.float32), spread[j * per : (j + 1) * per]], axis=1)
        summed = summed + (pltpu.roll(part, wide - j, 1) if j else part)
    own_buf[y, :, :length] = summed[:, LANES:].astype(jnp.bfloat16)
    halo_out[...] = jnp.where(
        iota((per, LANES), 1) < EDGE, summed[:, LANES : 2 * LANES], summed[:, :LANES]
    ).astype(jnp.bfloat16)

    pl.semaphore_wait(barrier, 2 * (RING - 1) + jnp.where(first, 0, 1))

    def lag_copy(d, source):
        g = lax.rem(z + d, RING)
        return pltpu.make_async_remote_copy(
            src_ref=lag_out.at[g],
            dst_ref=lags.at[source],
            send_sem=send_lag.at[d],
            recv_sem=recv_lag.at[source],
            device_id=(along_z(d), tm),
            device_id_type=MESH,
        )

    def own_copy(d, source):
        return pltpu.make_async_remote_copy(
            src_ref=own_buf.at[y],
            dst_ref=own_buf.at[source],
            send_sem=send_own.at[d],
            recv_sem=recv_own.at[source],
            device_id=(along_y(d), tm),
            device_id_type=MESH,
        )

    def hop_copy():
        return pltpu.make_async_remote_copy(
            src_ref=halo_out,
            dst_ref=halo_in,
            send_sem=send_edge.at[1],
            recv_sem=recv_edge.at[1],
            device_id=(sub, tm - 1),
            device_id_type=MESH,
        )

    @pl.when(tm > 0)
    def _():
        hop_copy().start()

    for d in FAR_FIRST:
        lag_copy(d, z).start()

    @pl.when(last)
    def _():
        own_buf[y, :, length:] = jnp.zeros((per, LANES), jnp.bfloat16)

    @pl.when(jnp.logical_not(last))
    def _():
        hop_copy().wait_recv()
        halo = halo_in[...].astype(jnp.float32)
        edge = jnp.where(iota((per, LANES), 1) >= EDGE, halo, 0.0)
        tail = own_buf[y, :, length - LANES : length].astype(jnp.float32) + edge
        own_buf[y, :, length - LANES : length] = tail.astype(jnp.bfloat16)
        own_buf[y, :, length:] = halo_in[...]

    for d in FAR_FIRST:
        own_copy(d, y).start()

    rows = RING * per
    for d in NEAR_FIRST:
        lag_copy(d, lax.rem(z + d, RING)).wait_recv()
    table = lags[...].reshape(RING * dms, rows).astype(jnp.float32).T.astype(jnp.bfloat16)

    for d in NEAR_FIRST:
        own_copy(d, lax.rem(y + d, RING)).wait_recv()
    turned[...] = own_buf[...].reshape(rows, wide).astype(jnp.float32).T

    def part_copy(t, d, source):
        return pltpu.make_async_remote_copy(
            src_ref=part_buf.at[t, lax.rem(z + d, RING)],
            dst_ref=sum_buf.at[t, source],
            send_sem=send_part.at[t * RING + d],
            recv_sem=recv_part.at[t * RING + source],
            device_id=(along_z(d), tm),
            device_id_type=MESH,
        )

    def edge_copy():
        return pltpu.make_async_remote_copy(
            src_ref=edge_out,
            dst_ref=edge_in,
            send_sem=send_edge.at[0],
            recv_sem=recv_edge.at[0],
            device_id=(sub, tm - 1),
            device_id_type=MESH,
        )

    tiles = length // LANES

    masks, windows = [], []
    for j in range(OMAX + 1):
        masks.append(jnp.where(table == jnp.bfloat16(j), jnp.bfloat16(1), jnp.bfloat16(0)))
        windows.append(turned[j : j + length, :].astype(jnp.bfloat16))
    total = jnp.dot(
        jnp.concatenate(windows, axis=1),
        jnp.concatenate(masks, axis=0),
        preferred_element_type=jnp.float32,
    )
    for t in range(tiles):
        tile = total[t * LANES : (t + 1) * LANES].T
        part_buf[t] = tile.astype(jnp.bfloat16).reshape(RING, dms, LANES)
        for d in FAR_FIRST:
            part_copy(t, d, z).start()
        sum_buf[t, z] = part_buf[t, z]

    def finish(t):
        for d in NEAR_FIRST:
            part_copy(t, d, lax.rem(z + d, RING)).wait_recv()
        added = sum_buf[t, 0].astype(jnp.float32)
        for g in range(1, RING):
            added = added + sum_buf[t, g].astype(jnp.float32)
        return (added * scale).astype(jnp.bfloat16)

    start = finish(0)
    edge_out[...] = start

    @pl.when(tm > 0)
    def _():
        edge_copy().start()

    out_ref[:, :LANES] = start
    for t in range(1, tiles):
        out_ref[:, t * LANES : (t + 1) * LANES] = finish(t)

    @pl.when(last)
    def _():
        edge_in[...] = jnp.zeros((dms, LANES), jnp.bfloat16)

    @pl.when(jnp.logical_not(last))
    def _():
        edge_copy().wait_recv()

    out_ref[:, length:] = edge_in[...]

    for d in NEAR_FIRST:
        own_copy(d, y).wait_send()
        lag_copy(d, z).wait_send()
        for t in range(tiles):
            part_copy(t, d, z).wait_send()

    @pl.when(tm > 0)
    def _():
        hop_copy().wait_send()
        edge_copy().wait_send()


def boxcar_kernel(widths_ref, series_ref, out_ref, woven):
    length = out_ref.shape[1]
    count = widths_ref.shape[0]
    dms = series_ref.shape[0]
    tiles = length // LANES
    spans = [series_ref[:, h * LANES : (h + 2) * LANES] for h in range(tiles)]
    spans = jnp.concatenate(spans, axis=0)
    lag = iota((2 * LANES, LANES), 0) - iota((2 * LANES, LANES), 1)
    lag = jnp.where(lag < 0, WMAX, lag)
    for i in range(count):
        width = widths_ref[i]
        window = jnp.where(lag < width, 1.0, 0.0).astype(jnp.bfloat16)
        total = jnp.dot(spans, window, preferred_element_type=jnp.float32)
        total = total / jnp.sqrt(jnp.full((1, LANES), width, jnp.int32).astype(jnp.float32))
        for h in range(tiles):
            woven[h, pl.ds(i, dms, stride=count), :] = total[h * dms : (h + 1) * dms]
    for h in range(tiles):
        out_ref[:, h * LANES : (h + 1) * LANES] = woven[h]


def solution(mesh):
    blocks = mesh.shape["tm"]

    def per_device(data, delays, offsets, widths):
        _, chans, length = data.shape
        dms, nsub = offsets.shape
        groups = lax.axis_size("sub")
        per = nsub // groups
        scale = 1.0 / math.sqrt(chans * groups)
        vmem = pl.BlockSpec(memory_space=pltpu.VMEM)
        bf16 = jnp.bfloat16
        dma = pltpu.SemaphoreType.DMA((RING,))
        series = pl.pallas_call(
            functools.partial(dedisperse_kernel, scale, blocks),
            out_shape=jax.ShapeDtypeStruct((dms, length + LANES), bf16),
            in_specs=[pl.BlockSpec(memory_space=pl.ANY)] * 3,
            out_specs=vmem,
            scratch_shapes=[
                pltpu.VMEM((chans, length), bf16),
                pltpu.VMEM((1, chans), jnp.int32),
                pltpu.VMEM((dms, nsub), jnp.int32),
                pltpu.VMEM((RING, dms, LANES), bf16),
                pltpu.VMEM((RING, dms, LANES), bf16),
                pltpu.VMEM((RING, per, length + LANES), bf16),
                pltpu.VMEM((per, LANES), bf16),
                pltpu.VMEM((per, LANES), bf16),
                pltpu.VMEM((length + LANES, RING * per), jnp.float32),
                pltpu.VMEM((length // LANES, RING, dms, LANES), bf16),
                pltpu.VMEM((length // LANES, RING, dms, LANES), bf16),
                pltpu.VMEM((dms, LANES), bf16),
                pltpu.VMEM((dms, LANES), bf16),
            ]
            + [dma] * 4
            + [pltpu.SemaphoreType.DMA((RING * (length // LANES),))] * 2
            + [pltpu.SemaphoreType.DMA((2,))] * 2
            + [pltpu.SemaphoreType.DMA((3,))],
            compiler_params=pltpu.CompilerParams(collective_id=0, has_side_effects=True),
        )(data[0], delays[None, :], offsets)
        count = widths.shape[0]
        out = pl.pallas_call(
            boxcar_kernel,
            out_shape=jax.ShapeDtypeStruct((dms * count, length), jnp.float32),
            in_specs=[pl.BlockSpec(memory_space=pltpu.SMEM), vmem],
            out_specs=vmem,
            scratch_shapes=[pltpu.VMEM((length // LANES, dms * count, LANES), jnp.float32)],
        )(widths, series)
        return out.reshape(dms, 1, count, length)

    placed = (P(None, "sub", "tm"), P("sub"), P("sub", None), P())
    return jax.shard_map(
        per_device,
        mesh=mesh,
        in_specs=placed,
        out_specs=P("sub", None, None, "tm"),
        check_vma=False,
    )
```

```python
import functools
import math

import jax
import jax.numpy as jnp
from jax import lax
from jax.experimental import pallas as pl
from jax.experimental.pallas import tpu as pltpu
from jax.sharding import PartitionSpec as P

WMAX = 128
DCH = 16
OMAX = 96
RING = 8
LANES = 128
EDGE = 112
MESH = pl.DeviceIdType.MESH
FAR_FIRST = (4, 3, 5, 2, 6, 1, 7)
NEAR_FIRST = (1, 7, 2, 6, 3, 5, 4)


def iota(shape, dim):
    return lax.broadcasted_iota(jnp.int32, shape, dim)


def dedisperse_kernel(
    scale,
    blocks,
    data_hbm,
    delays_hbm,
    offsets_hbm,
    out_ref,
    data_ref,
    delays_ref,
    offsets_ref,
    lag_out,
    lags,
    own_buf,
    halo_out,
    halo_buf,
    turned,
    part_buf,
    sum_buf,
    edge_out,
    edge_in,
    send_own,
    recv_own,
    send_halo,
    recv_halo,
    send_lag,
    recv_lag,
    send_part,
    recv_part,
    send_edge,
    recv_edge,
    load,
    ready,
):
    sub = lax.axis_index("sub")
    tm = lax.axis_index("tm")
    z, y = sub // RING, sub % RING
    chans, length = data_ref.shape
    per = own_buf.shape[1]
    dms = lag_out.shape[1]
    first, last = tm == 0, tm == blocks - 1

    def along_y(d):
        return z * RING + lax.rem(y + d, RING)

    def along_z(d):
        return lax.rem(z + d, RING) * RING + y

    barrier = pltpu.get_barrier_semaphore()

    def fetch(i, source, target):
        return pltpu.make_async_copy(source, target, load.at[i])

    fetch(0, data_hbm, data_ref).start()
    fetch(1, delays_hbm, delays_ref).start()
    fetch(2, offsets_hbm, offsets_ref).start()

    for d in FAR_FIRST:
        pl.semaphore_signal(barrier, inc=1, device_id=(along_y(d), tm), device_id_type=MESH)
        pl.semaphore_signal(barrier, inc=1, device_id=(along_z(d), tm), device_id_type=MESH)

    @pl.when(jnp.logical_not(last))
    def _():
        pl.semaphore_signal(barrier, inc=1, device_id=(sub, tm + 1), device_id_type=MESH)

    @pl.when(tm > 0)
    def _():
        pl.semaphore_signal(barrier, inc=1, device_id=(sub, tm - 1), device_id_type=MESH)

    fetch(2, offsets_hbm, offsets_ref).wait()
    for g in range(RING):
        lag_out[g] = offsets_ref[:, g * LANES : (g + 1) * LANES].astype(jnp.float32).astype(jnp.bfloat16)
    lags[z] = lag_out[z]

    fetch(0, data_hbm, data_ref).wait()
    fetch(1, delays_hbm, delays_ref).wait()
    pick, chan = iota((DCH * per, chans), 0), iota((DCH * per, chans), 1)
    same = jnp.logical_and(chan // (chans // per) == pick % per, delays_ref[...] == pick // per)
    spread = jnp.dot(
        jnp.where(same, 1.0, 0.0).astype(jnp.bfloat16), data_ref[...], preferred_element_type=jnp.float32
    )
    wide = length + LANES
    summed = jnp.zeros((per, wide), jnp.float32)
    for j in range(DCH):
        part = jnp.concatenate([jnp.zeros((per, LANES), jnp.float32), spread[j * per : (j + 1) * per]], axis=1)
        summed = summed + (pltpu.roll(part, wide - j, 1) if j else part)
    own_buf[y] = summed[:, LANES:].astype(jnp.bfloat16)
    halo_out[...] = jnp.where(
        iota((per, LANES), 1) < EDGE, summed[:, LANES : 2 * LANES], summed[:, :LANES]
    ).astype(jnp.bfloat16)

    pl.semaphore_wait(barrier, 2 * (RING - 1) + jnp.where(first, 0, 1) + jnp.where(last, 0, 1))

    @pl.when(jnp.logical_not(last))
    def _():
        pl.semaphore_signal(ready, inc=1, device_id=(sub, tm + 1), device_id_type=MESH)

    def lag_copy(d, source):
        g = lax.rem(z + d, RING)
        return pltpu.make_async_remote_copy(
            src_ref=lag_out.at[g],
            dst_ref=lags.at[source],
            send_sem=send_lag.at[d],
            recv_sem=recv_lag.at[source],
            device_id=(along_z(d), tm),
            device_id_type=MESH,
        )

    def own_copy(d, source):
        return pltpu.make_async_remote_copy(
            src_ref=own_buf.at[y],
            dst_ref=own_buf.at[source],
            send_sem=send_own.at[d],
            recv_sem=recv_own.at[source],
            device_id=(along_y(d), tm),
            device_id_type=MESH,
        )

    def halo_copy(d, source):
        return pltpu.make_async_remote_copy(
            src_ref=halo_out,
            dst_ref=halo_buf.at[source],
            send_sem=send_halo.at[d],
            recv_sem=recv_halo.at[source],
            device_id=(along_y(d), tm - 1),
            device_id_type=MESH,
        )

    for d in FAR_FIRST:
        own_copy(d, y).start()
        lag_copy(d, z).start()

    @pl.when(tm > 0)
    def _():
        pl.semaphore_wait(ready, 1)
        for d in FAR_FIRST + (0,):
            halo_copy(d, y).start()

    @pl.when(last)
    def _():
        halo_buf[...] = jnp.zeros(halo_buf.shape, halo_buf.dtype)

    rows = RING * per
    for d in NEAR_FIRST:
        lag_copy(d, lax.rem(z + d, RING)).wait_recv()
    table = lags[...].reshape(RING * dms, rows).astype(jnp.float32).T.astype(jnp.bfloat16)

    for d in NEAR_FIRST:
        own_copy(d, lax.rem(y + d, RING)).wait_recv()
    turned[:length] = own_buf[...].reshape(rows, length).astype(jnp.float32).T

    def part_copy(t, d, source):
        return pltpu.make_async_remote_copy(
            src_ref=part_buf.at[t, lax.rem(z + d, RING)],
            dst_ref=sum_buf.at[t, source],
            send_sem=send_part.at[t * RING + d],
            recv_sem=recv_part.at[t * RING + source],
            device_id=(along_z(d), tm),
            device_id_type=MESH,
        )

    def edge_copy():
        return pltpu.make_async_remote_copy(
            src_ref=edge_out,
            dst_ref=edge_in,
            send_sem=send_edge.at[0],
            recv_sem=recv_edge.at[0],
            device_id=(sub, tm - 1),
            device_id_type=MESH,
        )

    def add_halo():
        @pl.when(jnp.logical_not(last))
        def _():
            for d in (0,) + NEAR_FIRST:
                halo_copy(d, lax.rem(y + d, RING)).wait_recv()

        halo = halo_buf[...].reshape(rows, LANES).astype(jnp.float32)
        edge = jnp.where(iota((rows, LANES), 1) >= EDGE, halo, 0.0)
        tail = own_buf[:, :, length - LANES :].reshape(rows, LANES).astype(jnp.float32) + edge
        turned[length - LANES : length] = tail.astype(jnp.bfloat16).astype(jnp.float32).T
        turned[length:] = halo.T

    tiles = length // LANES

    def tile(t, carry):
        pl.when(t == tiles - 1)(add_halo)
        masks, windows = [], []
        for j in range(OMAX + 1):
            masks.append(jnp.where(table == jnp.bfloat16(j), jnp.bfloat16(1), jnp.bfloat16(0)))
            windows.append(turned[pl.ds(t * LANES + j, LANES), :].astype(jnp.bfloat16))
        total = jnp.dot(
            jnp.concatenate(windows, axis=1),
            jnp.concatenate(masks, axis=0),
            preferred_element_type=jnp.float32,
        )
        part_buf[t] = total.T.astype(jnp.bfloat16).reshape(RING, dms, LANES)
        for d in FAR_FIRST:
            part_copy(t, d, z).start()

        sum_buf[t, z] = part_buf[t, z]
        return carry

    lax.fori_loop(0, tiles, tile, 0)

    def finish(t):
        for d in NEAR_FIRST:
            part_copy(t, d, lax.rem(z + d, RING)).wait_recv()
        added = sum_buf[t, 0].astype(jnp.float32)
        for g in range(1, RING):
            added = added + sum_buf[t, g].astype(jnp.float32)
        return (added * scale).astype(jnp.bfloat16)

    start = finish(0)
    edge_out[...] = start

    @pl.when(tm > 0)
    def _():
        edge_copy().start()

    out_ref[:, :LANES] = start
    for t in range(1, tiles):
        out_ref[:, t * LANES : (t + 1) * LANES] = finish(t)

    @pl.when(last)
    def _():
        edge_in[...] = jnp.zeros((dms, LANES), jnp.bfloat16)

    @pl.when(jnp.logical_not(last))
    def _():
        edge_copy().wait_recv()

    out_ref[:, length:] = edge_in[...]

    for d in NEAR_FIRST:
        own_copy(d, y).wait_send()
        lag_copy(d, z).wait_send()
        for t in range(tiles):
            part_copy(t, d, z).wait_send()

    @pl.when(tm > 0)
    def _():
        for d in (0,) + NEAR_FIRST:
            halo_copy(d, y).wait_send()
        edge_copy().wait_send()


def boxcar_kernel(widths_ref, series_ref, out_ref, woven):
    length = out_ref.shape[1]
    count = widths_ref.shape[0]
    dms = series_ref.shape[0]
    tiles = length // LANES
    spans = [series_ref[:, h * LANES : (h + 2) * LANES] for h in range(tiles)]
    spans = jnp.concatenate(spans, axis=0)
    lag = iota((2 * LANES, LANES), 0) - iota((2 * LANES, LANES), 1)
    lag = jnp.where(lag < 0, WMAX, lag)
    for i in range(count):
        width = widths_ref[i]
        window = jnp.where(lag < width, 1.0, 0.0).astype(jnp.bfloat16)
        total = jnp.dot(spans, window, preferred_element_type=jnp.float32)
        total = total / jnp.sqrt(jnp.full((1, LANES), width, jnp.int32).astype(jnp.float32))
        for h in range(tiles):
            woven[h, pl.ds(i, dms, stride=count), :] = total[h * dms : (h + 1) * dms]
    for h in range(tiles):
        out_ref[:, h * LANES : (h + 1) * LANES] = woven[h]


def solution(mesh):
    blocks = mesh.shape["tm"]

    def per_device(data, delays, offsets, widths):
        _, chans, length = data.shape
        dms, nsub = offsets.shape
        groups = lax.axis_size("sub")
        per = nsub // groups
        scale = 1.0 / math.sqrt(chans * groups)
        vmem = pl.BlockSpec(memory_space=pltpu.VMEM)
        bf16 = jnp.bfloat16
        dma = pltpu.SemaphoreType.DMA((RING,))
        series = pl.pallas_call(
            functools.partial(dedisperse_kernel, scale, blocks),
            out_shape=jax.ShapeDtypeStruct((dms, length + LANES), bf16),
            in_specs=[pl.BlockSpec(memory_space=pl.ANY)] * 3,
            out_specs=vmem,
            scratch_shapes=[
                pltpu.VMEM((chans, length), bf16),
                pltpu.VMEM((1, chans), jnp.int32),
                pltpu.VMEM((dms, nsub), jnp.int32),
                pltpu.VMEM((RING, dms, LANES), bf16),
                pltpu.VMEM((RING, dms, LANES), bf16),
                pltpu.VMEM((RING, per, length), bf16),
                pltpu.VMEM((per, LANES), bf16),
                pltpu.VMEM((RING, per, LANES), bf16),
                pltpu.VMEM((length + LANES, RING * per), jnp.float32),
                pltpu.VMEM((length // LANES, RING, dms, LANES), bf16),
                pltpu.VMEM((length // LANES, RING, dms, LANES), bf16),
                pltpu.VMEM((dms, LANES), bf16),
                pltpu.VMEM((dms, LANES), bf16),
            ]
            + [dma] * 6
            + [pltpu.SemaphoreType.DMA((RING * (length // LANES),))] * 2
            + [pltpu.SemaphoreType.DMA((1,))] * 2
            + [pltpu.SemaphoreType.DMA((3,)), pltpu.SemaphoreType.REGULAR],
            compiler_params=pltpu.CompilerParams(collective_id=0, has_side_effects=True),
        )(data[0], delays[None, :], offsets)
        count = widths.shape[0]
        out = pl.pallas_call(
            boxcar_kernel,
            out_shape=jax.ShapeDtypeStruct((dms * count, length), jnp.float32),
            in_specs=[pl.BlockSpec(memory_space=pltpu.SMEM), vmem],
            out_specs=vmem,
            scratch_shapes=[pltpu.VMEM((length // LANES, dms * count, LANES), jnp.float32)],
        )(widths, series)
        return out.reshape(dms, 1, count, length)

    placed = (P(None, "sub", "tm"), P("sub"), P("sub", None), P())
    return jax.shard_map(
        per_device,
        mesh=mesh,
        in_specs=placed,
        out_specs=P("sub", None, None, "tm"),
        check_vma=False,
    )
```

```python
import functools
import math

import jax
import jax.numpy as jnp
from jax import lax
from jax.experimental import pallas as pl
from jax.experimental.pallas import tpu as pltpu
from jax.sharding import PartitionSpec as P

WMAX = 128
DCH = 16
OMAX = 96
RING = 8
LANES = 128
EDGE = 112
MESH = pl.DeviceIdType.MESH
FAR_FIRST = (4, 3, 5, 2, 6, 1, 7)
NEAR_FIRST = (1, 7, 2, 6, 3, 5, 4)


def iota(shape, dim):
    return lax.broadcasted_iota(jnp.int32, shape, dim)


def dedisperse_kernel(
    scale,
    blocks,
    data_hbm,
    delays_hbm,
    offsets_hbm,
    out_ref,
    data_ref,
    delays_ref,
    offsets_ref,
    lag_out,
    lags,
    own_buf,
    halo_out,
    halo_buf,
    turned,
    part_buf,
    sum_buf,
    edge_out,
    edge_in,
    send_own,
    recv_own,
    send_halo,
    recv_halo,
    send_lag,
    recv_lag,
    send_part,
    recv_part,
    send_edge,
    recv_edge,
    load,
):
    sub = lax.axis_index("sub")
    tm = lax.axis_index("tm")
    z, y = sub // RING, sub % RING
    chans, length = data_ref.shape
    per = own_buf.shape[1]
    dms = lag_out.shape[1]
    first, last = tm == 0, tm == blocks - 1

    def along_y(d):
        return z * RING + lax.rem(y + d, RING)

    def along_z(d):
        return lax.rem(z + d, RING) * RING + y

    barrier = pltpu.get_barrier_semaphore()

    def fetch(i, source, target):
        return pltpu.make_async_copy(source, target, load.at[i])

    fetch(0, data_hbm, data_ref).start()
    fetch(1, delays_hbm, delays_ref).start()
    fetch(2, offsets_hbm, offsets_ref).start()

    for d in FAR_FIRST:
        pl.semaphore_signal(barrier, inc=1, device_id=(along_y(d), tm), device_id_type=MESH)
        pl.semaphore_signal(barrier, inc=1, device_id=(along_z(d), tm), device_id_type=MESH)

    @pl.when(jnp.logical_not(last))
    def _():
        pl.semaphore_signal(barrier, inc=1, device_id=(sub, tm + 1), device_id_type=MESH)

    fetch(2, offsets_hbm, offsets_ref).wait()
    for g in range(RING):
        lag_out[g] = offsets_ref[:, g * LANES : (g + 1) * LANES].astype(jnp.float32).astype(jnp.bfloat16)
    lags[z] = lag_out[z]

    fetch(0, data_hbm, data_ref).wait()
    fetch(1, delays_hbm, delays_ref).wait()
    pick, chan = iota((DCH * per, chans), 0), iota((DCH * per, chans), 1)
    same = jnp.logical_and(chan // (chans // per) == pick % per, delays_ref[...] == pick // per)
    spread = jnp.dot(
        jnp.where(same, 1.0, 0.0).astype(jnp.bfloat16), data_ref[...], preferred_element_type=jnp.float32
    )
    wide = length + LANES
    summed = jnp.zeros((per, wide), jnp.float32)
    for j in range(DCH):
        part = jnp.concatenate([jnp.zeros((per, LANES), jnp.float32), spread[j * per : (j + 1) * per]], axis=1)
        summed = summed + (pltpu.roll(part, wide - j, 1) if j else part)
    own_buf[y] = summed[:, LANES:].astype(jnp.bfloat16)
    halo_out[...] = jnp.where(
        iota((per, LANES), 1) < EDGE, summed[:, LANES : 2 * LANES], summed[:, :LANES]
    ).astype(jnp.bfloat16)

    pl.semaphore_wait(barrier, 2 * (RING - 1) + jnp.where(first, 0, 1))

    def lag_copy(d, source):
        g = lax.rem(z + d, RING)
        return pltpu.make_async_remote_copy(
            src_ref=lag_out.at[g],
            dst_ref=lags.at[source],
            send_sem=send_lag.at[d],
            recv_sem=recv_lag.at[source],
            device_id=(along_z(d), tm),
            device_id_type=MESH,
        )

    def own_copy(d, source):
        return pltpu.make_async_remote_copy(
            src_ref=own_buf.at[y],
            dst_ref=own_buf.at[source],
            send_sem=send_own.at[d],
            recv_sem=recv_own.at[source],
            device_id=(along_y(d), tm),
            device_id_type=MESH,
        )

    def hop_copy():
        return pltpu.make_async_remote_copy(
            src_ref=halo_out,
            dst_ref=halo_buf.at[y],
            send_sem=send_edge.at[1],
            recv_sem=recv_edge.at[1],
            device_id=(sub, tm - 1),
            device_id_type=MESH,
        )

    def halo_copy(d, source):
        return pltpu.make_async_remote_copy(
            src_ref=halo_buf.at[y],
            dst_ref=halo_buf.at[source],
            send_sem=send_halo.at[d],
            recv_sem=recv_halo.at[source],
            device_id=(along_y(d), tm),
            device_id_type=MESH,
        )

    @pl.when(tm > 0)
    def _():
        hop_copy().start()

    for d in FAR_FIRST:
        own_copy(d, y).start()
        lag_copy(d, z).start()

    @pl.when(last)
    def _():
        halo_buf[...] = jnp.zeros(halo_buf.shape, halo_buf.dtype)

    @pl.when(jnp.logical_not(last))
    def _():
        hop_copy().wait_recv()
        for d in FAR_FIRST:
            halo_copy(d, y).start()

    rows = RING * per
    for d in NEAR_FIRST:
        lag_copy(d, lax.rem(z + d, RING)).wait_recv()
    table = lags[...].reshape(RING * dms, rows).astype(jnp.float32).T.astype(jnp.bfloat16)

    for d in NEAR_FIRST:
        own_copy(d, lax.rem(y + d, RING)).wait_recv()
    turned[:length] = own_buf[...].reshape(rows, length).astype(jnp.float32).T

    def part_copy(t, d, source):
        return pltpu.make_async_remote_copy(
            src_ref=part_buf.at[t, lax.rem(z + d, RING)],
            dst_ref=sum_buf.at[t, source],
            send_sem=send_part.at[t * RING + d],
            recv_sem=recv_part.at[t * RING + source],
            device_id=(along_z(d), tm),
            device_id_type=MESH,
        )

    def edge_copy():
        return pltpu.make_async_remote_copy(
            src_ref=edge_out,
            dst_ref=edge_in,
            send_sem=send_edge.at[0],
            recv_sem=recv_edge.at[0],
            device_id=(sub, tm - 1),
            device_id_type=MESH,
        )

    def add_halo():
        @pl.when(jnp.logical_not(last))
        def _():
            for d in NEAR_FIRST:
                halo_copy(d, lax.rem(y + d, RING)).wait_recv()

        halo = halo_buf[...].reshape(rows, LANES).astype(jnp.float32)
        edge = jnp.where(iota((rows, LANES), 1) >= EDGE, halo, 0.0)
        tail = own_buf[:, :, length - LANES :].reshape(rows, LANES).astype(jnp.float32) + edge
        turned[length - LANES : length] = tail.astype(jnp.bfloat16).astype(jnp.float32).T
        turned[length:] = halo.T

    tiles = length // LANES

    def tile(t, carry):
        pl.when(t == tiles - 1)(add_halo)
        masks, windows = [], []
        for j in range(OMAX + 1):
            masks.append(jnp.where(table == jnp.bfloat16(j), jnp.bfloat16(1), jnp.bfloat16(0)))
            windows.append(turned[pl.ds(t * LANES + j, LANES), :].astype(jnp.bfloat16))
        total = jnp.dot(
            jnp.concatenate(windows, axis=1),
            jnp.concatenate(masks, axis=0),
            preferred_element_type=jnp.float32,
        )
        part_buf[t] = total.T.astype(jnp.bfloat16).reshape(RING, dms, LANES)
        for d in FAR_FIRST:
            part_copy(t, d, z).start()

        sum_buf[t, z] = part_buf[t, z]
        return carry

    lax.fori_loop(0, tiles, tile, 0)

    def finish(t):
        for d in NEAR_FIRST:
            part_copy(t, d, lax.rem(z + d, RING)).wait_recv()
        added = sum_buf[t, 0].astype(jnp.float32)
        for g in range(1, RING):
            added = added + sum_buf[t, g].astype(jnp.float32)
        return (added * scale).astype(jnp.bfloat16)

    start = finish(0)
    edge_out[...] = start

    @pl.when(tm > 0)
    def _():
        edge_copy().start()

    out_ref[:, :LANES] = start
    for t in range(1, tiles):
        out_ref[:, t * LANES : (t + 1) * LANES] = finish(t)

    @pl.when(last)
    def _():
        edge_in[...] = jnp.zeros((dms, LANES), jnp.bfloat16)

    @pl.when(jnp.logical_not(last))
    def _():
        edge_copy().wait_recv()

    out_ref[:, length:] = edge_in[...]

    for d in NEAR_FIRST:
        own_copy(d, y).wait_send()
        lag_copy(d, z).wait_send()
        for t in range(tiles):
            part_copy(t, d, z).wait_send()

    @pl.when(jnp.logical_not(last))
    def _():
        for d in NEAR_FIRST:
            halo_copy(d, y).wait_send()

    @pl.when(tm > 0)
    def _():
        hop_copy().wait_send()
        edge_copy().wait_send()


def boxcar_kernel(widths_ref, series_ref, out_ref, woven):
    length = out_ref.shape[1]
    count = widths_ref.shape[0]
    dms = series_ref.shape[0]
    tiles = length // LANES
    spans = [series_ref[:, h * LANES : (h + 2) * LANES] for h in range(tiles)]
    spans = jnp.concatenate(spans, axis=0)
    lag = iota((2 * LANES, LANES), 0) - iota((2 * LANES, LANES), 1)
    lag = jnp.where(lag < 0, WMAX, lag)
    for i in range(count):
        width = widths_ref[i]
        window = jnp.where(lag < width, 1.0, 0.0).astype(jnp.bfloat16)
        total = jnp.dot(spans, window, preferred_element_type=jnp.float32)
        total = total / jnp.sqrt(jnp.full((1, LANES), width, jnp.int32).astype(jnp.float32))
        for h in range(tiles):
            woven[h, pl.ds(i, dms, stride=count), :] = total[h * dms : (h + 1) * dms]
    for h in range(tiles):
        out_ref[:, h * LANES : (h + 1) * LANES] = woven[h]


def solution(mesh):
    blocks = mesh.shape["tm"]

    def per_device(data, delays, offsets, widths):
        _, chans, length = data.shape
        dms, nsub = offsets.shape
        groups = lax.axis_size("sub")
        per = nsub // groups
        scale = 1.0 / math.sqrt(chans * groups)
        vmem = pl.BlockSpec(memory_space=pltpu.VMEM)
        bf16 = jnp.bfloat16
        dma = pltpu.SemaphoreType.DMA((RING,))
        series = pl.pallas_call(
            functools.partial(dedisperse_kernel, scale, blocks),
            out_shape=jax.ShapeDtypeStruct((dms, length + LANES), bf16),
            in_specs=[pl.BlockSpec(memory_space=pl.ANY)] * 3,
            out_specs=vmem,
            scratch_shapes=[
                pltpu.VMEM((chans, length), bf16),
                pltpu.VMEM((1, chans), jnp.int32),
                pltpu.VMEM((dms, nsub), jnp.int32),
                pltpu.VMEM((RING, dms, LANES), bf16),
                pltpu.VMEM((RING, dms, LANES), bf16),
                pltpu.VMEM((RING, per, length), bf16),
                pltpu.VMEM((per, LANES), bf16),
                pltpu.VMEM((RING, per, LANES), bf16),
                pltpu.VMEM((length + LANES, RING * per), jnp.float32),
                pltpu.VMEM((length // LANES, RING, dms, LANES), bf16),
                pltpu.VMEM((length // LANES, RING, dms, LANES), bf16),
                pltpu.VMEM((dms, LANES), bf16),
                pltpu.VMEM((dms, LANES), bf16),
            ]
            + [dma] * 6
            + [pltpu.SemaphoreType.DMA((RING * (length // LANES),))] * 2
            + [pltpu.SemaphoreType.DMA((2,))] * 2
            + [pltpu.SemaphoreType.DMA((3,))],
            compiler_params=pltpu.CompilerParams(collective_id=0, has_side_effects=True, vmem_limit_bytes=16 * 2**20),
        )(data[0], delays[None, :], offsets)
        count = widths.shape[0]
        out = pl.pallas_call(
            boxcar_kernel,
            out_shape=jax.ShapeDtypeStruct((dms * count, length), jnp.float32),
            in_specs=[pl.BlockSpec(memory_space=pltpu.SMEM), vmem],
            out_specs=vmem,
            compiler_params=pltpu.CompilerParams(vmem_limit_bytes=16 * 2**20),
            scratch_shapes=[pltpu.VMEM((length // LANES, dms * count, LANES), jnp.float32)],
        )(widths, series)
        return out.reshape(dms, 1, count, length)

    placed = (P(None, "sub", "tm"), P("sub"), P("sub", None), P())
    return jax.shard_map(
        per_device,
        mesh=mesh,
        in_specs=placed,
        out_specs=P("sub", None, None, "tm"),
        check_vma=False,
    )
```
